32 devices in a mesh: seq: 4 (over y, core), head: 2 (over x), wa: 4 (over z).
Axes of the slice: x: 2, y: 2, z: 4, core: 2. Of those that a mesh axis runs over, the one named last changes fastest.
Arguments:
- tokens: bfloat16 [4, 2048, 1024], P('wa', ('seq', 'head')), may hold values from -6 to 6
- prenorm: float32 [1024], replicated, may hold values from 0.5 to 1.5
- joint_weight: bfloat16 [2048, 1024], P('wa'), may hold values from -1 to 1, as said below
- query_gain: float32 [64], replicated, may hold values from 0.5 to 1.5
- key_gain: float32 [64], replicated, may hold values from 0.6 to 22, as said below
- output_weight: bfloat16 [1024, 1024], P('wa'), may hold values from -6 to 6
- midnorm: float32 [1024], replicated, may hold values from 0.5 to 1.5
- gate_weight: bfloat16 [4608, 1024], P('wa'), may hold values from -0.1875 to 0.1875
- up_weight: bfloat16 [4608, 1024], P('wa'), may hold values from -0.1875 to 0.1875
- down_weight: bfloat16 [4608, 1024], P('wa'), may hold values from -0.09375 to 0.09375
- cotangent: bfloat16 [4, 2048, 1024], P('wa', ('seq', 'head')), may hold values from -6 to 6
Outputs:
- block_out: bfloat16 [4, 2048, 1024], P('wa', ('seq', 'head'))
- grad_tokens: float32 [4, 2048, 1024], P('wa', ('seq', 'head'))
- grad_prenorm: float32 [1024], P('wa')
- grad_joint: float32 [2048, 1024], P('wa')
- grad_query: float32 [64], P('wa')
- grad_key: float32 [64], P('wa')
- grad_output: float32 [1024, 1024], P('wa')
- grad_midnorm: float32 [1024], P('wa')
- grad_gate: float32 [4608, 1024], P('wa')
- grad_up: float32 [4608, 1024], P('wa')
- grad_down: float32 [4608, 1024], P('wa')
The draws below stay inside these ranges and needn't reach their ends.
Inputs may be any that keep to these rules, and one draw needn't show every extreme that they name: `joint_weight`: entries have a spread of about 1 / sqrt(1024). `key_gain`: the key norm's gains are positive.
All inputs are finite; a program needn't handle non-finite values.
Results may differ from the reference program's by a relative error of at most 0.04.
The reference program's roundings to bfloat16 on the way count: a program that leaves them out, or rounds other values in their place, can miss the bound.
Values may be sent and summed in bfloat16 or wider, within the bound.
No kernel may reach another device: no remote copies, remote signals or barrier semaphores. Data moves between devices by JAX's collectives and lax.ppermute only.
A program may use at most 192 MiB of HBM per device.

```python
import jax
import jax.numpy as jnp
from jax import lax

D = 1024
H = 16
KVH = 8
HD = 64
FF = 4608
HQ = 1024
QKVW = 2048
LEN = 2048
NSEQ = 4


def draw_tokens(key, part):
    base_key = jax.random.fold_in(key, 101)
    return jnp.clip(jax.random.normal(base_key, (NSEQ, LEN, D), jnp.float32), -6.0, 6.0).astype(jnp.bfloat16)


def draw_joint_weight(key, part):
    spread = float(D) ** (-0.5)
    query_key = jax.random.fold_in(key, 201)
    return (jnp.clip(jax.random.normal(query_key, (QKVW, D), jnp.float32), -6.0, 6.0) * spread).astype(jnp.bfloat16)


def draw_key_gain(key, part):
    base = jax.random.uniform(jax.random.fold_in(key, 301), (HD,), jnp.float32, 0.0, 1.0)
    return 0.6 + 0.9 * base


def draw_output_weight(key, part):
    draws = jnp.clip(jax.random.normal(jax.random.fold_in(key, 401), (D, HQ), jnp.float32), -6.0, 6.0)
    return (draws * float(max(1, HQ * 16 // LEN)) ** (-0.5)).astype(jnp.bfloat16)


def levels(key, extent, shards, smallest, high):
    gain, own = 1.0, jax.random.fold_in(key, 6)
    for dim, blocks in shards:
        steps = jnp.exp(jax.random.uniform(jax.random.fold_in(own, dim), (blocks,), jnp.float32, smallest / len(shards), high / len(shards)))
        gain = gain * jnp.repeat(steps, extent[dim] // blocks).reshape([-1 if axis == dim else 1 for axis in range(len(extent))])
    return gain


def scatter_about(rng, dims, scale, most, shards=(), held_as=jnp.bfloat16):
    level = levels(rng, dims, shards, -0.22, 0.18) if shards else 1.0
    values = jax.random.normal(rng, dims, jnp.float32) * scale * level
    return jnp.minimum(jnp.maximum(values, -most), most).astype(held_as)


def setup_inputs(seed: int = 0) -> dict:
    key_list = jax.random.split(jax.random.key(seed), 12)
    return {
        "tokens": draw_tokens(jax.random.fold_in(key_list[11], 71), 0),
        "prenorm": jnp.clip(1.0 + 0.1 * jax.random.normal(key_list[1], (D,), jnp.float32), 0.5, 1.5),
        "joint_weight": draw_joint_weight(jax.random.fold_in(key_list[11], 71), 0),
        "query_gain": jnp.clip(1.0 + 0.1 * jax.random.normal(key_list[3], (HD,), jnp.float32), 0.5, 1.5),
        "key_gain": draw_key_gain(jax.random.fold_in(key_list[11], 71), 0),
        "output_weight": draw_output_weight(jax.random.fold_in(key_list[11], 71), 0),
        "midnorm": jnp.clip(1.0 + 0.1 * jax.random.normal(key_list[6], (D,), jnp.float32), 0.5, 1.5),
        "gate_weight": scatter_about(key_list[7], (FF, D), D ** -0.5, 0.1875, ((0, 4),)),
        "up_weight": scatter_about(key_list[8], (FF, D), D ** -0.5, 0.1875, ((0, 4),)),
        "down_weight": scatter_about(key_list[9], (FF, D), FF ** -0.5, 0.09375, ((0, 4),)),
        "cotangent": scatter_about(key_list[10], (NSEQ, LEN, D), 1.0, 6.0, ((0, 4), (1, 8))),
    }


EPS = 1e-05
THETA = 1000000.0
BLOCK = 512

def inverse_rms(values):
    return lax.rsqrt(lax.optimization_barrier(jnp.mean(values * values, axis=-1, keepdims=True)) + EPS)

def rope_tables(positions, head_depth):
    half_depth = head_depth // 2
    frequency = THETA ** (-(jnp.arange(half_depth).astype(jnp.float32) * 2.0 / head_depth))
    angles = positions.astype(jnp.float32)[:, None] * frequency[None, :]
    return (jnp.cos(angles), jnp.sin(angles))

def rotate(values, cosine, sine):
    half_depth = values.shape[-1] // 2
    front_half = values[..., :half_depth]
    back_half = values[..., half_depth:]
    return jnp.concatenate([front_half * cosine - back_half * sine, back_half * cosine + front_half * sine], axis=-1)

def norm_back(grad_normal, normal, inverse):
    return inverse * (grad_normal - normal * lax.optimization_barrier(jnp.mean(grad_normal * normal, axis=-1, keepdims=True)))

def barrier_round(values):
    return lax.optimization_barrier(values.astype(jnp.bfloat16)).astype(jnp.float32)

def reference(tokens, prenorm, joint_weight, query_gain, key_gain, output_weight, midnorm, gate_weight, up_weight, down_weight, cotangent):
    group_size = H // KVH
    score_scale = HD ** (-0.5)
    grad_scale = (NSEQ * LEN) ** (-0.5)
    block = BLOCK if LEN % BLOCK == 0 else LEN
    block_count = LEN // block
    cosine, sine = rope_tables(jnp.arange(LEN), HD)
    cos_query = cosine[:, None, None, :]
    sin_query = sine[:, None, None, :]
    cos_key = cosine[:, None, :]
    sin_key = sine[:, None, :]
    key_pos = jnp.arange(LEN)
    query_cols = H * HD
    key_end = query_cols + KVH * HD
    block_ids = jnp.arange(block_count).astype(jnp.int32)

    def one_sequence(totals, paired):
        seq_tokens, seq_cot = paired
        resid = seq_tokens.astype(jnp.float32)
        pre_inverse = inverse_rms(resid)
        pre_normal = resid * pre_inverse
        normed = (pre_normal * prenorm).astype(jnp.bfloat16)
        joint = jnp.dot(normed, joint_weight.T, preferred_element_type=jnp.float32)
        raw_query = joint[:, :query_cols].reshape(LEN, KVH, group_size, HD)
        raw_key = joint[:, query_cols:key_end].reshape(LEN, KVH, HD)
        values = joint[:, key_end:].reshape(LEN, KVH, HD).astype(jnp.bfloat16)
        query_inverse = inverse_rms(raw_query)
        query_normal = raw_query * query_inverse
        key_inverse = inverse_rms(raw_key)
        key_normal = raw_key * key_inverse
        queries = rotate(query_normal * query_gain, cos_query, sin_query).astype(jnp.bfloat16)
        keys_rot = rotate(key_normal * key_gain, cos_key, sin_key).astype(jnp.bfloat16)
        keys_wide = keys_rot.astype(jnp.float32)
        values_wide = values.astype(jnp.float32)

        def masked_scores(row_start, query_block):
            scores = jnp.einsum('qkgd,jkd->kgqj', query_block.astype(jnp.float32), keys_wide) * score_scale
            rows_pos = row_start + jnp.arange(block)
            return jnp.where(key_pos[None, :] <= rows_pos[:, None], scores, -jnp.inf)

        def forward_block(unused, block_no):
            row_start = block_no * block
            query_block = lax.dynamic_slice_in_dim(queries, row_start, block, 0)
            scores = masked_scores(row_start, query_block)
            row_peak = lax.optimization_barrier(jnp.max(scores, axis=-1, keepdims=True))
            log_norm = row_peak + jnp.log(lax.optimization_barrier(jnp.sum(jnp.exp(scores - row_peak), axis=-1, keepdims=True)))
            weights = jnp.exp(scores - log_norm).astype(jnp.bfloat16)
            attended = jnp.einsum('kgqj,jkd->qkgd', weights.astype(jnp.float32), values_wide)
            return (unused, (attended.astype(jnp.bfloat16), log_norm))
        unused_carry, (attended, log_norms) = lax.scan(forward_block, None, block_ids)
        attended = attended.reshape(LEN, KVH, group_size, HD)
        attn_rows = attended.reshape(LEN, H * HD)
        middle = resid + jnp.dot(attn_rows, output_weight.T, preferred_element_type=jnp.float32)
        mid_inverse = inverse_rms(middle)
        mid_normal = middle * mid_inverse
        hidden_in = (mid_normal * midnorm).astype(jnp.bfloat16)
        gate_pre = jnp.dot(hidden_in, gate_weight.T, preferred_element_type=jnp.float32)
        up_pre = jnp.dot(hidden_in, up_weight.T, preferred_element_type=jnp.float32)
        sigma = jax.nn.sigmoid(gate_pre)
        activ = (gate_pre * sigma * up_pre).astype(jnp.bfloat16)
        block_out = (middle + jnp.dot(activ, down_weight, preferred_element_type=jnp.float32)).astype(jnp.bfloat16)
        act_grad = jnp.dot(seq_cot, down_weight.T, preferred_element_type=jnp.float32)
        gate_back = (act_grad * up_pre * sigma * (1.0 + gate_pre * (1.0 - sigma))).astype(jnp.bfloat16)
        up_back = (act_grad * gate_pre * sigma).astype(jnp.bfloat16)
        hidden_grad = jnp.dot(gate_back, gate_weight, preferred_element_type=jnp.float32) + jnp.dot(up_back, up_weight, preferred_element_type=jnp.float32)
        middle_grad = seq_cot.astype(jnp.float32) + norm_back(hidden_grad * midnorm, mid_normal, mid_inverse)
        middle_low = middle_grad.astype(jnp.bfloat16)
        attended_grad = jnp.dot(middle_low, output_weight, preferred_element_type=jnp.float32).astype(jnp.bfloat16).reshape(LEN, KVH, group_size, HD)

        def backward_block(carry, block_no):
            key_acc, value_acc = carry
            row_start = block_no * block
            query_block = lax.dynamic_slice_in_dim(queries, row_start, block, 0)
            grad_block = lax.dynamic_slice_in_dim(attended_grad, row_start, block, 0).astype(jnp.float32)
            out_block = lax.dynamic_slice_in_dim(attended, row_start, block, 0).astype(jnp.float32)
            scores = masked_scores(row_start, query_block)
            probs = jnp.exp(scores - log_norms[block_no])
            delta = jnp.einsum('qkgd,qkgd->kgq', grad_block, out_block)[..., None]
            dot_grad = jnp.einsum('qkgd,jkd->kgqj', grad_block, values_wide)
            score_grad = barrier_round(probs * (dot_grad - delta))
            probs_low = barrier_round(probs)
            value_acc = value_acc + jnp.einsum('kgqj,qkgd->jkd', probs_low, grad_block)
            key_acc = key_acc + jnp.einsum('kgqj,qkgd->jkd', score_grad, query_block.astype(jnp.float32)) * score_scale
            query_grad = (jnp.einsum('kgqj,jkd->qkgd', score_grad, keys_wide) * score_scale).astype(jnp.bfloat16)
            return ((key_acc, value_acc), query_grad)
        zero_kv = jnp.zeros((LEN, KVH, HD), jnp.float32)
        (key_acc, value_acc), query_grads = lax.scan(backward_block, (zero_kv, zero_kv), block_ids)
        query_wide = lax.optimization_barrier(query_grads).reshape(LEN, KVH, group_size, HD).astype(jnp.float32)
        query_scaled = rotate(query_wide, cos_query, -sin_query)
        query_gain_grad = lax.optimization_barrier(jnp.sum(query_scaled * query_normal, axis=(0, 1, 2)))
        query_raw = norm_back(query_scaled * query_gain, query_normal, query_inverse)
        key_scaled = rotate(barrier_round(key_acc), cos_key, -sin_key)
        key_gain_grad = lax.optimization_barrier(jnp.sum(key_scaled * key_normal, axis=(0, 1)))
        key_raw = norm_back(key_scaled * key_gain, key_normal, key_inverse)
        joint_back = jnp.concatenate([query_raw.reshape(LEN, H * HD).astype(jnp.bfloat16), key_raw.reshape(LEN, KVH * HD).astype(jnp.bfloat16), value_acc.reshape(LEN, KVH * HD).astype(jnp.bfloat16)], axis=-1)
        normed_grad = jnp.dot(joint_back, joint_weight, preferred_element_type=jnp.float32)
        token_grad = middle_grad + norm_back(normed_grad * prenorm, pre_normal, pre_inverse)
        grads = (jnp.dot(joint_back.T, normed, preferred_element_type=jnp.float32), jnp.dot(middle_low.T, attn_rows, preferred_element_type=jnp.float32), jnp.dot(gate_back.T, hidden_in, preferred_element_type=jnp.float32), jnp.dot(up_back.T, hidden_in, preferred_element_type=jnp.float32), jnp.dot(activ.T, seq_cot, preferred_element_type=jnp.float32), lax.optimization_barrier(jnp.sum(normed_grad * pre_normal, axis=0)), lax.optimization_barrier(jnp.sum(hidden_grad * mid_normal, axis=0)), query_gain_grad, key_gain_grad)
        totals = tuple((member + extra for member, extra in zip(totals, grads)))
        return (totals, (block_out, token_grad))
    start_totals = (jnp.zeros((QKVW, D), jnp.float32), jnp.zeros((D, HQ), jnp.float32), jnp.zeros((FF, D), jnp.float32), jnp.zeros((FF, D), jnp.float32), jnp.zeros((FF, D), jnp.float32), jnp.zeros((D,), jnp.float32), jnp.zeros((D,), jnp.float32), jnp.zeros((HD,), jnp.float32), jnp.zeros((HD,), jnp.float32))
    totals, (block_out, grad_tokens) = lax.scan(one_sequence, start_totals, (tokens, cotangent))
    scaled = tuple((member * grad_scale for member in totals))
    return (block_out, grad_tokens, scaled[5], scaled[0], scaled[7], scaled[8], scaled[1], scaled[6], scaled[2], scaled[3], scaled[4])
```

```python
import jax
import jax.numpy as jnp
from jax import lax
from jax.experimental import pallas as pl
from jax.experimental.pallas import tpu as pltpu
from jax.sharding import PartitionSpec as P

H = 16
KVH = 8
HD = 64


EPS = 1e-05
THETA = 1000000.0
BLOCK = 512
TEAM = ("seq", "head")
BF = jnp.bfloat16
F32 = jnp.float32
INTERPRET = False


def inverse_rms(values):
    return lax.rsqrt(jnp.mean(values * values, axis=-1, keepdims=True) + EPS)


def rope_tables(positions, head_depth):
    half_depth = head_depth // 2
    frequency = THETA ** (-(jnp.arange(half_depth).astype(jnp.float32) * 2.0 / head_depth))
    angles = positions.astype(jnp.float32)[:, None] * frequency[None, :]
    return (jnp.cos(angles), jnp.sin(angles))


def rotate(values, cosine, sine):
    half_depth = values.shape[-1] // 2
    front_half = values[..., :half_depth]
    back_half = values[..., half_depth:]
    return jnp.concatenate(
        [front_half * cosine - back_half * sine, back_half * cosine + front_half * sine], axis=-1
    )


def norm_back(grad_normal, normal, inverse):
    return inverse * (grad_normal - normal * jnp.mean(grad_normal * normal, axis=-1, keepdims=True))


def per_device_runs(
    tokens,
    prenorm,
    joint_weight,
    query_gain,
    key_gain,
    output_weight,
    midnorm,
    gate_weight,
    up_weight,
    down_weight,
    cotangent,
):
    seq_local, local_rows, model_width = tokens.shape
    seq_count = lax.axis_size("seq")
    head_count = lax.axis_size("head")
    shard_count = lax.axis_size("wa")
    group_size = H // KVH
    local_heads = KVH // head_count
    run_rows = local_rows * head_count
    block = BLOCK
    query_blocks = run_rows // block
    score_scale = HD ** (-0.5)
    grad_scale = float(shard_count * seq_local * local_rows * seq_count * head_count) ** (-0.5)
    seq_index = lax.axis_index("seq")
    head_index = lax.axis_index("head")
    positions = (seq_index * head_count + head_index) * local_rows + jnp.arange(local_rows)
    run_start = seq_index * run_rows
    cosine, sine = rope_tables(positions, HD)
    cos_query = cosine[None, :, None, None, :]
    sin_query = sine[None, :, None, None, :]
    cos_key = cosine[None, :, None, :]
    sin_key = sine[None, :, None, :]
    query_cols = H * HD
    key_end = query_cols + KVH * HD
    gathered_joint, gathered_output = (
        lax.all_gather(joint_weight, "wa", axis=0, tiled=True),
        lax.all_gather(output_weight, "wa", axis=0, tiled=True),
    )
    resid = tokens.astype(jnp.float32)
    pre_inverse = inverse_rms(resid)
    pre_normal = resid * pre_inverse
    normed = (pre_normal * prenorm).astype(jnp.bfloat16)
    joint = jnp.einsum("std,ed->ste", normed, gathered_joint, preferred_element_type=jnp.float32)
    raw_query = joint[..., :query_cols].reshape(seq_local, local_rows, KVH, group_size, HD)
    raw_key = joint[..., query_cols:key_end].reshape(seq_local, local_rows, KVH, HD)
    values = joint[..., key_end:].reshape(seq_local, local_rows, KVH, HD).astype(jnp.bfloat16)
    query_inverse = inverse_rms(raw_query)
    query_normal = raw_query * query_inverse
    key_inverse = inverse_rms(raw_key)
    key_normal = raw_key * key_inverse
    queries = rotate(query_normal * query_gain, cos_query, sin_query).astype(jnp.bfloat16)
    keys_rot = rotate(key_normal * key_gain, cos_key, sin_key).astype(jnp.bfloat16)
    packed = jnp.concatenate(
        [queries.reshape(seq_local, local_rows, KVH, group_size * HD), keys_rot, values], axis=-1
    )
    by_head = lax.all_to_all(packed, "head", split_axis=2, concat_axis=1, tiled=True)
    head_queries = by_head[..., : group_size * HD].reshape(
        seq_local, run_rows, local_heads, group_size, HD
    )
    key_value = by_head[..., group_size * HD :]
    all_kv = lax.all_gather(key_value, "seq", axis=1, tiled=True)
    all_keys = all_kv[..., :HD]
    all_values = all_kv[..., HD:]

    def masked_scores(query_block, key_block, query_start, key_start):
        scores = (
            jnp.einsum(
                "sqkgd,sjkd->skgqj", query_block, key_block, preferred_element_type=jnp.float32
            )
            * score_scale
        )
        rows_pos = query_start + jnp.arange(block)
        cols_pos = key_start + jnp.arange(block)
        return jnp.where(cols_pos[None, :] <= rows_pos[:, None], scores, -jnp.inf)

    def needed_blocks(query_start):
        return (query_start + block - 1) // block + 1

    stat_shape = (seq_local, local_heads, group_size, block, 1)

    def forward_block(block_no, carry):
        out_buffer, norm_buffer = carry
        row_start = block_no * block
        query_block = lax.dynamic_slice_in_dim(head_queries, row_start, block, 1)
        query_pos = run_start + row_start
        key_count = needed_blocks(query_pos)

        def stats_step(key_no, running):
            row_peak, row_total = running
            col_start = key_no * block
            key_block = lax.dynamic_slice_in_dim(all_keys, col_start, block, 1)
            scores = masked_scores(query_block, key_block, query_pos, col_start)
            new_peak = jnp.maximum(row_peak, jnp.max(scores, axis=-1, keepdims=True))
            row_total = row_total * jnp.exp(row_peak - new_peak) + jnp.sum(
                jnp.exp(scores - new_peak), axis=-1, keepdims=True
            )
            return (new_peak, row_total)

        row_peak, row_total = lax.fori_loop(
            0,
            key_count,
            stats_step,
            (jnp.full(stat_shape, -jnp.inf, jnp.float32), jnp.zeros(stat_shape, jnp.float32)),
        )
        log_norm = row_peak + jnp.log(row_total)

        def value_step(key_no, value_sum):
            col_start = key_no * block
            key_block = lax.dynamic_slice_in_dim(all_keys, col_start, block, 1)
            value_block = lax.dynamic_slice_in_dim(all_values, col_start, block, 1)
            weights = jnp.exp(
                masked_scores(query_block, key_block, query_pos, col_start) - log_norm
            ).astype(jnp.bfloat16)
            return value_sum + jnp.einsum(
                "skgqj,sjkd->sqkgd", weights, value_block, preferred_element_type=jnp.float32
            )

        value_sum = lax.fori_loop(
            0,
            key_count,
            value_step,
            jnp.zeros((seq_local, block, local_heads, group_size, HD), jnp.float32),
        )
        out_buffer = lax.dynamic_update_slice_in_dim(
            out_buffer, value_sum.astype(jnp.bfloat16), row_start, 1
        )
        norm_buffer = lax.dynamic_update_slice_in_dim(norm_buffer, log_norm, row_start, 3)
        return (out_buffer, norm_buffer)

    out_buffer, norm_buffer = lax.fori_loop(
        0,
        query_blocks,
        forward_block,
        (
            jnp.zeros((seq_local, run_rows, local_heads, group_size, HD), jnp.bfloat16),
            jnp.zeros((seq_local, local_heads, group_size, run_rows, 1), jnp.float32),
        ),
    )
    attended_heads = out_buffer.reshape(seq_local, run_rows, local_heads, group_size * HD)
    attn_rows = lax.all_to_all(
        attended_heads, "head", split_axis=1, concat_axis=2, tiled=True
    ).reshape(seq_local, local_rows, H * HD)
    middle = resid + jnp.einsum(
        "ste,de->std", attn_rows, gathered_output, preferred_element_type=jnp.float32
    )
    mid_inverse = inverse_rms(middle)
    mid_normal = middle * mid_inverse
    hidden_in = (mid_normal * midnorm).astype(jnp.bfloat16)
    all_hidden, all_cot = (
        lax.all_gather(hidden_in, "wa", axis=0, tiled=True),
        lax.all_gather(cotangent, "wa", axis=0, tiled=True),
    )
    gate_pre = jnp.einsum(
        "std,fd->stf", all_hidden, gate_weight, preferred_element_type=jnp.float32
    )
    up_pre = jnp.einsum("std,fd->stf", all_hidden, up_weight, preferred_element_type=jnp.float32)
    sigma = jax.nn.sigmoid(gate_pre)
    activ = (gate_pre * sigma * up_pre).astype(jnp.bfloat16)
    ffn_part = jnp.einsum("stf,fd->std", activ, down_weight, preferred_element_type=jnp.float32)
    ffn_out = lax.psum_scatter(ffn_part, "wa", scatter_dimension=0, tiled=True)
    block_out = (middle + ffn_out).astype(jnp.bfloat16)
    act_grad = jnp.einsum("std,fd->stf", all_cot, down_weight, preferred_element_type=jnp.float32)
    gate_back = (act_grad * up_pre * sigma * (1.0 + gate_pre * (1.0 - sigma))).astype(jnp.bfloat16)
    up_back = (act_grad * gate_pre * sigma).astype(jnp.bfloat16)
    grad_down = (
        jnp.einsum("stf,std->fd", activ, all_cot, preferred_element_type=jnp.float32) * grad_scale
    )
    grad_gate = (
        jnp.einsum("stf,std->fd", gate_back, all_hidden, preferred_element_type=jnp.float32)
        * grad_scale
    )
    grad_up = (
        jnp.einsum("stf,std->fd", up_back, all_hidden, preferred_element_type=jnp.float32)
        * grad_scale
    )
    hidden_part = jnp.einsum(
        "stf,fd->std", gate_back, gate_weight, preferred_element_type=jnp.float32
    ) + jnp.einsum("stf,fd->std", up_back, up_weight, preferred_element_type=jnp.float32)
    hidden_grad = lax.psum_scatter(hidden_part, "wa", scatter_dimension=0, tiled=True)
    grad_midnorm = jnp.sum(hidden_grad * mid_normal, axis=(0, 1)) * grad_scale
    middle_grad = cotangent.astype(jnp.float32) + norm_back(
        hidden_grad * midnorm, mid_normal, mid_inverse
    )
    middle_low = middle_grad.astype(jnp.bfloat16)
    grad_output = (
        jnp.einsum("std,ste->de", middle_low, attn_rows, preferred_element_type=jnp.float32)
        * grad_scale
    )
    attended_grad = (
        jnp.einsum("std,de->ste", middle_low, gathered_output, preferred_element_type=jnp.float32)
        .astype(jnp.bfloat16)
        .reshape(seq_local, local_rows, KVH, group_size * HD)
    )
    grad_heads = lax.all_to_all(
        attended_grad, "head", split_axis=2, concat_axis=1, tiled=True
    ).reshape(seq_local, run_rows, local_heads, group_size, HD)
    delta_all = jnp.einsum(
        "sqkgd,sqkgd->skgq", grad_heads, out_buffer, preferred_element_type=jnp.float32
    )[..., None]

    def backward_block(block_no, carry):
        kv_grads, query_grads = carry
        row_start = block_no * block
        query_block = lax.dynamic_slice_in_dim(head_queries, row_start, block, 1)
        grad_block = lax.dynamic_slice_in_dim(grad_heads, row_start, block, 1)
        norm_block = lax.dynamic_slice_in_dim(norm_buffer, row_start, block, 3)
        delta_block = lax.dynamic_slice_in_dim(delta_all, row_start, block, 3)
        query_pos = run_start + row_start

        def key_step(key_no, inner):
            kv_inner, query_sum = inner
            col_start = key_no * block
            key_block = lax.dynamic_slice_in_dim(all_keys, col_start, block, 1)
            value_block = lax.dynamic_slice_in_dim(all_values, col_start, block, 1)
            probs = jnp.exp(
                masked_scores(query_block, key_block, query_pos, col_start) - norm_block
            )
            dot_grad = jnp.einsum(
                "sqkgd,sjkd->skgqj", grad_block, value_block, preferred_element_type=jnp.float32
            )
            score_grad = (probs * (dot_grad - delta_block)).astype(jnp.bfloat16)
            value_term = jnp.einsum(
                "skgqj,sqkgd->sjkd",
                probs.astype(jnp.bfloat16),
                grad_block,
                preferred_element_type=jnp.float32,
            )
            key_term = (
                jnp.einsum(
                    "skgqj,sqkgd->sjkd", score_grad, query_block, preferred_element_type=jnp.float32
                )
                * score_scale
            )
            query_sum = (
                query_sum
                + jnp.einsum(
                    "skgqj,sjkd->sqkgd", score_grad, key_block, preferred_element_type=jnp.float32
                )
                * score_scale
            )
            previous = lax.dynamic_slice_in_dim(kv_inner, col_start, block, 1)
            kv_inner = lax.dynamic_update_slice_in_dim(
                kv_inner, previous + jnp.concatenate([key_term, value_term], axis=-1), col_start, 1
            )
            return (kv_inner, query_sum)

        kv_grads, query_sum = lax.fori_loop(
            0,
            needed_blocks(query_pos),
            key_step,
            (kv_grads, jnp.zeros((seq_local, block, local_heads, group_size, HD), jnp.float32)),
        )
        query_grads = lax.dynamic_update_slice_in_dim(
            query_grads, query_sum.astype(jnp.bfloat16), row_start, 1
        )
        return (kv_grads, query_grads)

    kv_grads, query_grads = lax.fori_loop(
        0,
        query_blocks,
        backward_block,
        (
            jnp.zeros((seq_local, seq_count * run_rows, local_heads, 2 * HD), jnp.float32),
            jnp.zeros((seq_local, run_rows, local_heads, group_size, HD), jnp.bfloat16),
        ),
    )
    kv_sums = lax.psum_scatter(kv_grads, "seq", scatter_dimension=1, tiled=True).astype(
        jnp.bfloat16
    )
    back_pack = jnp.concatenate(
        [query_grads.reshape(seq_local, run_rows, local_heads, group_size * HD), kv_sums], axis=-1
    )
    back_tokens = lax.all_to_all(back_pack, "head", split_axis=1, concat_axis=2, tiled=True)
    query_wide = (
        back_tokens[..., : group_size * HD]
        .reshape(seq_local, local_rows, KVH, group_size, HD)
        .astype(jnp.float32)
    )
    key_wide = back_tokens[..., group_size * HD : group_size * HD + HD].astype(jnp.float32)
    value_back = back_tokens[..., group_size * HD + HD :]
    query_scaled = rotate(query_wide, cos_query, -sin_query)
    grad_query_all = jnp.sum(query_scaled * query_normal, axis=(0, 1, 2, 3)) * grad_scale
    query_raw = norm_back(query_scaled * query_gain, query_normal, query_inverse)
    key_scaled = rotate(key_wide, cos_key, -sin_key)
    grad_key_all = jnp.sum(key_scaled * key_normal, axis=(0, 1, 2)) * grad_scale
    key_raw = norm_back(key_scaled * key_gain, key_normal, key_inverse)
    joint_back = jnp.concatenate(
        [
            query_raw.reshape(seq_local, local_rows, H * HD).astype(jnp.bfloat16),
            key_raw.reshape(seq_local, local_rows, KVH * HD).astype(jnp.bfloat16),
            value_back.reshape(seq_local, local_rows, KVH * HD),
        ],
        axis=-1,
    )
    normed_grad = jnp.einsum(
        "ste,ed->std", joint_back, gathered_joint, preferred_element_type=jnp.float32
    )
    grad_joint_all = (
        jnp.einsum("ste,std->ed", joint_back, normed, preferred_element_type=jnp.float32)
        * grad_scale
    )
    grad_prenorm_all = jnp.sum(normed_grad * pre_normal, axis=(0, 1)) * grad_scale
    grad_tokens = middle_grad + norm_back(normed_grad * prenorm, pre_normal, pre_inverse)
    joint_share, output_share, prenorm_share, query_share, key_share, midnorm_share = (
        lax.psum_scatter(grad_joint_all, "wa", scatter_dimension=0, tiled=True),
        lax.psum_scatter(grad_output, "wa", scatter_dimension=0, tiled=True),
        lax.psum_scatter(grad_prenorm_all, "wa", scatter_dimension=0, tiled=True),
        lax.psum_scatter(grad_query_all, "wa", scatter_dimension=0, tiled=True),
        lax.psum_scatter(grad_key_all, "wa", scatter_dimension=0, tiled=True),
        lax.psum_scatter(grad_midnorm, "wa", scatter_dimension=0, tiled=True),
    )
    (
        joint_total,
        output_total,
        prenorm_total,
        query_total,
        key_total,
        midnorm_total,
        gate_total,
        up_total,
        down_total,
    ) = lax.psum(
        (
            joint_share,
            output_share,
            prenorm_share,
            query_share,
            key_share,
            midnorm_share,
            grad_gate,
            grad_up,
            grad_down,
        ),
        ("seq", "head"),
    )
    return (
        block_out,
        grad_tokens,
        prenorm_total,
        joint_total,
        query_total,
        key_total,
        output_total,
        midnorm_total,
        gate_total,
        up_total,
        down_total,
    )


def split(values, axis):
    return jnp.split(values, 2, axis=axis)


def rotate_rows(values, cosine, sine):
    front_half, back_half = split(values, 0)
    return jnp.concatenate(
        [front_half * cosine - back_half * sine, back_half * cosine + front_half * sine], axis=0
    )


def inverse_rms_rows(values):
    return lax.rsqrt(jnp.mean(values * values, axis=0, keepdims=True) + EPS)


def norm_back_rows(grad_normal, normal, inverse):
    return inverse * (grad_normal - normal * jnp.mean(grad_normal * normal, axis=0, keepdims=True))


def turned(values):
    return jnp.transpose(values.astype(F32)).astype(BF)


def dot(left, right):
    return jnp.dot(left, right, preferred_element_type=F32)


def attend_kernel(
    joint_ref,
    cos_ref,
    sin_ref,
    query_gain_ref,
    key_gain_ref,
    out_ref,
    norm_ref,
    query_ref,
    key_ref,
    key_rows_ref,
    value_ref,
    key_s,
    value_rows_s,
    score_s,
):
    step = pl.program_id(0)
    rows = joint_ref.shape[2]
    heads = query_ref.shape[2] // rows
    cosine, sine = cos_ref[0], sin_ref[0]
    query_gain, key_gain = query_gain_ref[...], key_gain_ref[...]
    raw = joint_ref[0]
    parts = []
    for head in range(heads):
        raw_query = raw[head * HD : (head + 1) * HD]
        normal = raw_query * inverse_rms_rows(raw_query)
        parts.append(rotate_rows(normal * query_gain, cosine, sine).astype(BF))
    scale = jnp.asarray(HD ** (-0.5), BF)
    queries = jnp.concatenate(parts, axis=1) * scale
    raw_key = raw[heads * HD : (heads + 1) * HD]
    key_normal = raw_key * inverse_rms_rows(raw_key)
    keys_f32 = rotate_rows(key_normal * key_gain, cosine, sine)
    values_f32 = raw[(heads + 1) * HD :]
    keys = jnp.transpose(keys_f32).astype(BF)
    value_rows = values_f32.astype(BF)
    query_ref[0] = queries
    key_ref[0] = keys
    key_rows_ref[0] = keys_f32.astype(BF)
    value_ref[0] = jnp.transpose(values_f32).astype(BF)
    key_s[step] = keys
    value_rows_s[step] = value_rows
    lanes = heads * rows

    def fold(scores, reducer):
        return reducer(scores.reshape(rows // 8, 8, lanes), axis=0)

    key_pos = lax.broadcasted_iota(jnp.int32, (rows, rows), 0)
    query_pos = lax.broadcasted_iota(jnp.int32, (rows, rows), 1)
    allowed = jnp.concatenate([key_pos <= query_pos] * heads, axis=1)
    own = jnp.where(allowed, dot(keys, queries), -jnp.inf)
    score_s[step] = own

    def peak_step(block_no, peak):
        scores = dot(key_s[block_no], queries)
        score_s[block_no] = scores
        return jnp.maximum(peak, fold(scores, jnp.max))

    peak = lax.fori_loop(0, step, peak_step, fold(own, jnp.max))
    peak = jnp.max(peak, axis=0, keepdims=True)

    def sum_step(block_no, carry):
        total, value_sum = carry
        weights = jnp.exp(score_s[block_no] - peak)
        total = total + fold(weights, jnp.sum)
        value_sum = value_sum + dot(value_rows_s[block_no], weights.astype(BF))
        return total, value_sum

    total, value_sum = lax.fori_loop(
        0, step + 1, sum_step, (jnp.zeros((8, lanes), F32), jnp.zeros((HD, lanes), F32))
    )
    total = jnp.sum(total, axis=0, keepdims=True)
    attended = (value_sum / total).astype(BF)
    norm_ref[0] = peak + jnp.log(total)
    for head in range(heads):
        out_ref[0, head * HD : (head + 1) * HD] = attended[:, head * rows : (head + 1) * rows]


def attend(joint_rows, cosine, sine, query_gain, key_gain):
    blocks, width, rows = joint_rows.shape
    heads = width // HD - 2
    lanes = heads * rows
    whole = lambda shape: pl.BlockSpec(shape, lambda i: (0,) * len(shape))
    one = lambda *shape: pl.BlockSpec((1,) + shape, lambda i: (i,) + (0,) * len(shape))
    struct = jax.ShapeDtypeStruct
    return pl.pallas_call(
        attend_kernel,
        grid=(blocks,),
        in_specs=[
            one(width, rows),
            one(HD // 2, rows),
            one(HD // 2, rows),
            whole((HD, 1)),
            whole((HD, 1)),
        ],
        out_specs=[
            one(heads * HD, rows),
            one(1, lanes),
            one(HD, lanes),
            one(rows, HD),
            one(HD, rows),
            one(rows, HD),
        ],
        out_shape=[
            struct((blocks, heads * HD, rows), BF),
            struct((blocks, 1, lanes), F32),
            struct((blocks, HD, lanes), BF),
            struct((blocks, rows, HD), BF),
            struct((blocks, HD, rows), BF),
            struct((blocks, rows, HD), BF),
        ],
        scratch_shapes=[
            pltpu.VMEM((blocks, rows, HD), BF),
            pltpu.VMEM((blocks, HD, rows), BF),
            pltpu.VMEM((blocks, rows, lanes), F32),
        ],
        interpret=INTERPRET,
        name="attend",
    )(joint_rows, cosine, sine, query_gain, key_gain)


def attend_back_kernel(
    grad_ref,
    out_ref,
    norm_ref,
    query_ref,
    key_ref,
    key_rows_ref,
    value_ref,
    joint_ref,
    cos_ref,
    sin_ref,
    query_gain_ref,
    key_gain_ref,
    back_ref,
    query_gain_grad_ref,
    key_gain_grad_ref,
    key_acc,
    value_acc,
    gain_acc,
):
    step = pl.program_id(0)
    rows = grad_ref.shape[2]
    heads = query_ref.shape[2] // rows
    lanes = heads * rows

    @pl.when(step == 0)
    def clear():
        key_acc[...] = jnp.zeros(key_acc.shape, F32)
        value_acc[...] = jnp.zeros(value_acc.shape, F32)
        gain_acc[...] = jnp.zeros(gain_acc.shape, F32)

    def side_by_side(ref):
        return jnp.concatenate([ref[0, h * HD : (h + 1) * HD] for h in range(heads)], axis=1)

    grads = side_by_side(grad_ref)
    delta = jnp.sum(grads.astype(F32) * side_by_side(out_ref).astype(F32), axis=0, keepdims=True)
    norm = norm_ref[0]
    queries = query_ref[0]
    query_cols = turned(queries)
    grad_cols = turned(grads)
    key_pos = lax.broadcasted_iota(jnp.int32, (rows, rows), 0)
    query_pos = lax.broadcasted_iota(jnp.int32, (rows, rows), 1)
    allowed = jnp.concatenate([key_pos <= query_pos] * heads, axis=1)

    def block_step(block_no, query_sum, mask):
        probs = jnp.exp(dot(key_ref[block_no], queries) - norm)
        if mask:
            probs = jnp.where(allowed, probs, 0.0)
        score_grad = (probs * (dot(value_ref[block_no], grads) - delta)).astype(BF)
        value_acc[block_no] += dot(probs.astype(BF), grad_cols)
        key_acc[block_no] += dot(score_grad, query_cols)
        return query_sum + dot(key_rows_ref[block_no], score_grad)

    query_sum = block_step(step, jnp.zeros((HD, lanes), F32), True)
    query_sum = lax.fori_loop(0, step, lambda b, s: block_step(b, s, False), query_sum)
    query_grad = (query_sum * HD ** (-0.5)).astype(BF).astype(F32)
    cosine, sine = cos_ref[step], sin_ref[step]
    query_gain = query_gain_ref[...]
    for head in range(heads):
        raw = joint_ref[step, head * HD : (head + 1) * HD]
        inverse = inverse_rms_rows(raw)
        normal = raw * inverse
        scaled = rotate_rows(query_grad[:, head * rows : (head + 1) * rows], cosine, -sine)
        gain_acc[0] += scaled * normal
        back_ref[step, head * HD : (head + 1) * HD] = norm_back_rows(
            scaled * query_gain, normal, inverse
        ).astype(BF)

    @pl.when(step == pl.num_programs(0) - 1)
    def finish():
        key_gain = key_gain_ref[...]

        def finish_block(block_no, carry):
            raw = joint_ref[block_no, heads * HD : (heads + 1) * HD]
            inverse = inverse_rms_rows(raw)
            normal = raw * inverse
            key_grad = jnp.transpose(key_acc[block_no]).astype(BF).astype(F32)
            scaled = rotate_rows(key_grad, cos_ref[block_no], -sin_ref[block_no])
            gain_acc[1] += scaled * normal
            back_ref[block_no, heads * HD : (heads + 1) * HD] = norm_back_rows(
                scaled * key_gain, normal, inverse
            ).astype(BF)
            back_ref[block_no, (heads + 1) * HD :] = jnp.transpose(value_acc[block_no]).astype(BF)
            return carry

        lax.fori_loop(0, pl.num_programs(0), finish_block, 0)
        query_gain_grad_ref[...] = jnp.sum(gain_acc[0], axis=1, keepdims=True)
        key_gain_grad_ref[...] = jnp.sum(gain_acc[1], axis=1, keepdims=True)


def attend_back(grads, attended, saved, joint_rows, cosine, sine, query_gain, key_gain):
    norm, queries, keys, key_rows, values = saved
    blocks, width, rows = joint_rows.shape
    heads = width // HD - 2
    lanes = heads * rows
    whole = lambda shape: pl.BlockSpec(shape, lambda i: (0,) * len(shape))
    one = lambda *shape: pl.BlockSpec((1,) + shape, lambda i: (i,) + (0,) * len(shape))
    struct = jax.ShapeDtypeStruct
    return pl.pallas_call(
        attend_back_kernel,
        grid=(blocks,),
        in_specs=[
            one(heads * HD, rows),
            one(heads * HD, rows),
            one(1, lanes),
            one(HD, lanes),
            whole(keys.shape),
            whole(key_rows.shape),
            whole(values.shape),
            whole(joint_rows.shape),
            whole(cosine.shape),
            whole(sine.shape),
            whole((HD, 1)),
            whole((HD, 1)),
        ],
        out_specs=[whole(joint_rows.shape), whole((HD, 1)), whole((HD, 1))],
        out_shape=[struct(joint_rows.shape, BF), struct((HD, 1), F32), struct((HD, 1), F32)],
        scratch_shapes=[
            pltpu.VMEM((blocks, rows, HD), F32),
            pltpu.VMEM((blocks, rows, HD), F32),
            pltpu.VMEM((2, HD, rows), F32),
        ],
        interpret=INTERPRET,
        name="attend_back",
    )(
        grads, attended, norm, queries, keys, key_rows, values,
        joint_rows, cosine, sine, query_gain, key_gain,
    )


def per_device_heads(
    tokens,
    prenorm,
    joint_weight,
    query_gain,
    key_gain,
    output_weight,
    midnorm,
    gate_weight,
    up_weight,
    down_weight,
    cotangent,
):
    _, local_rows, model_width = tokens.shape
    head_count = lax.axis_size("head")
    shard_count = lax.axis_size("wa")
    team = lax.axis_size("seq") * head_count
    group_size = H // KVH
    head_width = (group_size + 2) * HD
    grad_scale = float(shard_count * local_rows * team) ** (-0.5)
    place = lax.axis_index(TEAM)
    plane = lax.axis_index("wa")
    near = head_count
    far = [1 << b for b in range(team.bit_length() - 1) if 1 << b != near]

    def swap(values, mask):
        return lax.ppermute(values, TEAM, [(i, i ^ mask) for i in range(team)])

    def bit(mask):
        return (place // mask) % 2

    order = [0] + list(range(1, shard_count, 2)) + list(range(2, shard_count, 2))[::-1]
    ring_pairs = [(order[i], order[(i + 1) % shard_count]) for i in range(shard_count)]

    def pick(table, index):
        return sum(jnp.where(index == k, entry, 0) for k, entry in enumerate(table))

    ring_place = pick([order.index(k) for k in range(shard_count)], plane)

    def ring(values):
        return lax.ppermute(values, "wa", ring_pairs)

    def owner(slot):
        return pick(order, (ring_place - slot) % shard_count)

    def ring_gather(values):
        slots = [values]
        for _ in range(shard_count - 1):
            slots.append(ring(slots[-1]))
        return slots

    def ring_reduce(slots):
        total = slots[1].astype(BF)
        for slot in list(range(2, shard_count)) + [0]:
            total = ring(total).astype(F32) + slots[slot]
            if slot:
                total = total.astype(BF)
        return total

    def team_gather(tile):
        tiles = {0: tile}
        half = tile.shape[0] // 2
        first, second = far
        tiles[first] = swap(tile, first)
        tiles[second] = swap(tile, second)
        tiles[near] = swap(tile, near)
        top = swap(tiles[first][:half], second)
        bottom = swap(tiles[second][half:], first)
        tiles[first ^ second] = jnp.concatenate([top, bottom], axis=0)
        for mask in (first, second, first ^ second):
            tiles[mask ^ near] = swap(tiles[mask], near)
        return tiles

    def collect(tiles, axis=0):
        shape = list(tiles[0].shape)
        shape.insert(axis, team)
        buffer = jnp.zeros(shape, tiles[0].dtype)
        for mask, tile in tiles.items():
            buffer = lax.dynamic_update_slice_in_dim(
                buffer, jnp.expand_dims(tile, axis), place ^ mask, axis
            )
        return buffer

    def exchange(tiles):
        received = {0: lax.dynamic_index_in_dim(tiles, place, 0, keepdims=False)}
        for mask in range(1, team):
            received[mask] = swap(
                lax.dynamic_index_in_dim(tiles, place ^ mask, 0, keepdims=False), mask
            )
        return collect(received)

    def halve(values, mask):
        rows = values.shape[-2] // 2
        axis = values.ndim - 2
        kept = lax.dynamic_slice_in_dim(values, bit(mask) * rows, rows, axis)
        sent = lax.dynamic_slice_in_dim(values, (1 - bit(mask)) * rows, rows, axis)
        return (kept.astype(F32) + swap(sent, mask).astype(F32)).astype(BF)

    def join(values, mask):
        other = swap(values, mask)
        axis = values.ndim - 2
        return jnp.where(
            bit(mask) == 0,
            jnp.concatenate([values, other], axis=axis),
            jnp.concatenate([other, values], axis=axis),
        )

    def team_reduce(values):
        values = halve(values.astype(BF), near)
        left, right = split(values, values.ndim - 1)
        for first, second in (far, far[::-1]):
            left, right = halve(left, first), halve(right, second)
        return left, right

    def team_spread(left, right):
        for first, second in (far[::-1], far):
            left, right = join(left, first), join(right, second)
        return join(jnp.concatenate([left, right], axis=-1), near)

    def team_sum(values):
        return team_spread(*team_reduce(values))

    positions = jnp.arange(team * local_rows).astype(F32)
    half_depth = HD // 2
    frequency = THETA ** (-(jnp.arange(half_depth).astype(F32) * 2.0 / HD))
    angles = positions.reshape(team, 1, local_rows) * frequency[None, :, None]
    cosine, sine = jnp.cos(angles), jnp.sin(angles)
    query_gain_col, key_gain_col = query_gain[:, None], key_gain[:, None]

    shard_rows = joint_weight.shape[0]
    query_rows = group_size * HD
    query_shards = KVH * query_rows // shard_rows
    query_shard = place * query_rows // shard_rows
    query_offset = place * query_rows % shard_rows
    is_query = plane < query_shards
    pieces = [
        lax.dynamic_slice_in_dim(
            joint_weight, jnp.where(is_query, query_offset + k * HD, place * HD), HD, 0
        )
        for k in range(group_size)
    ]
    slots = jnp.concatenate(ring_gather(jnp.concatenate(pieces, axis=0)), axis=0)

    def slot_of(shard):
        return (ring_place - pick([order.index(k) for k in range(shard_count)], shard)) % shard_count

    head_weight = jnp.concatenate(
        [
            lax.dynamic_slice_in_dim(slots, slot_of(query_shard) * query_rows, query_rows, 0),
            lax.dynamic_slice_in_dim(slots, slot_of(query_shards) * query_rows, HD, 0),
            lax.dynamic_slice_in_dim(slots, slot_of(query_shards + 1) * query_rows, HD, 0),
        ],
        axis=0,
    )

    resid = tokens[0].astype(F32)
    pre_inverse = inverse_rms(resid)
    pre_normal = resid * pre_inverse
    normed = (pre_normal * prenorm).astype(BF)
    normed_tiles = team_gather(normed)
    joint_rows = collect(
        {
            mask: jnp.einsum("ed,td->et", head_weight, tile, preferred_element_type=F32)
            for mask, tile in normed_tiles.items()
        }
    )

    piece_rows = output_weight.shape[0] // team
    output_piece = lax.dynamic_slice_in_dim(output_weight, place * piece_rows, piece_rows, 0)
    output_slots = jnp.zeros((shard_count, piece_rows, model_width), BF)
    for slot, piece in enumerate(ring_gather(output_piece)):
        output_slots = lax.dynamic_update_slice_in_dim(output_slots, piece[None], owner(slot), 0)
    output_slots = output_slots.reshape(shard_count * piece_rows, model_width)
    output_slots, _ = lax.optimization_barrier((output_slots, normed_tiles[team - 1]))
    output_tiles = {
        mask: tile.reshape(shard_count, piece_rows, model_width)
        for mask, tile in team_gather(output_slots).items()
    }
    whole_output = collect(output_tiles, 1).reshape(-1, model_width)

    attended, *saved = attend(joint_rows, cosine, sine, query_gain_col, key_gain_col)
    attn_rows = exchange(attended).reshape(H * HD, local_rows)
    middle = resid + jnp.einsum("et,de->td", attn_rows, whole_output, preferred_element_type=F32)
    mid_inverse = inverse_rms(middle)
    mid_normal = middle * mid_inverse
    hidden_in = (mid_normal * midnorm).astype(BF)

    late_cot, late_weight, _ = lax.optimization_barrier((cotangent[0], head_weight, output_slots))
    cot_slots = ring_gather(late_cot)
    hidden_slots = ring_gather(hidden_in)
    joint_tiles = team_gather(late_weight)

    acts, gate_backs, up_backs, out_parts, hidden_parts = [], [], [], [], []
    for hidden, cot in zip(hidden_slots, cot_slots):
        gate_pre = jnp.einsum("td,fd->tf", hidden, gate_weight, preferred_element_type=F32)
        up_pre = jnp.einsum("td,fd->tf", hidden, up_weight, preferred_element_type=F32)
        act_grad = jnp.einsum("td,fd->tf", cot, down_weight, preferred_element_type=F32)
        sigma = jax.nn.sigmoid(gate_pre)
        acts.append((gate_pre * sigma * up_pre).astype(BF))
        gate_backs.append(
            (act_grad * up_pre * sigma * (1.0 + gate_pre * (1.0 - sigma))).astype(BF)
        )
        up_backs.append((act_grad * gate_pre * sigma).astype(BF))
        hidden_parts.append(dot(gate_backs[-1], gate_weight) + dot(up_backs[-1], up_weight))
        out_parts.append(dot(acts[-1], down_weight))
    hidden_grad = ring_reduce(hidden_parts)

    all_hidden = jnp.concatenate(hidden_slots, axis=0)
    all_cot = jnp.concatenate(cot_slots, axis=0)

    def weight_grad(backs, inputs):
        backs = jnp.concatenate(backs, axis=0)
        return jnp.einsum("tf,td->fd", backs, inputs, preferred_element_type=F32).astype(BF)

    down_total = team_sum(weight_grad(acts, all_cot)).astype(F32) * grad_scale
    gate_total = team_sum(weight_grad(gate_backs, all_hidden)).astype(F32) * grad_scale
    up_total = team_sum(weight_grad(up_backs, all_hidden)).astype(F32) * grad_scale

    cot = cotangent[0].astype(F32)
    middle_grad = cot + norm_back(hidden_grad * midnorm, mid_normal, mid_inverse)
    middle_low = middle_grad.astype(BF)
    attended_grad = jnp.einsum(
        "td,de->et", middle_low, whole_output, preferred_element_type=F32
    ).astype(BF)
    head_grads = exchange(attended_grad.reshape(team, query_rows, local_rows))
    back_rows, query_gain_part, key_gain_part = attend_back(
        head_grads, attended, saved, joint_rows, cosine, sine, query_gain_col, key_gain_col
    )

    out_parts[1], _ = lax.optimization_barrier((out_parts[1], hidden_grad))
    block_out = (middle + ring_reduce(out_parts)).astype(BF)

    output_part = jnp.einsum("td,et->de", middle_low, attn_rows, preferred_element_type=F32)
    output_part = output_part.reshape(shard_count, -1, H * HD)
    output_halves = [
        ring_reduce(
            [
                lax.dynamic_index_in_dim(part, owner(slot), 0, keepdims=False)
                for slot in range(shard_count)
            ]
        ).astype(BF)
        for part in team_reduce(output_part)
    ]
    output_total = team_spread(*output_halves).astype(F32) * grad_scale

    token_back = exchange(back_rows).reshape(KVH * head_width, local_rows)
    whole_joint = collect(joint_tiles).reshape(KVH * head_width, model_width)
    normed_grad = jnp.einsum("et,ed->td", token_back, whole_joint, preferred_element_type=F32)
    grad_tokens = middle_grad + norm_back(normed_grad * prenorm, pre_normal, pre_inverse)

    all_normed = collect(normed_tiles)
    head_part = jnp.einsum("uet,utd->ed", back_rows, all_normed, preferred_element_type=F32)
    head_part = head_part.astype(BF)
    head_total = ring_reduce(
        [
            lax.dynamic_slice_in_dim(
                head_part, jnp.where(owner(slot) < query_shards, 0, query_rows), query_rows, 0
            )
            for slot in range(shard_count)
        ]
    ).astype(BF)
    head_totals = collect(team_gather(head_total))
    per_shard = team // query_shards
    as_query = lax.dynamic_slice_in_dim(
        head_totals, jnp.minimum(plane, query_shards - 1) * per_shard, per_shard, 0
    ).reshape(shard_rows, model_width)
    as_key = lax.dynamic_slice_in_dim(
        head_totals, jnp.maximum(plane - query_shards, 0) * HD, HD, 1
    ).reshape(shard_rows, model_width)
    joint_total = jnp.where(is_query, as_query, as_key).astype(F32) * grad_scale

    small = lax.psum(
        jnp.concatenate(
            [
                jnp.sum(normed_grad * pre_normal, axis=0),
                jnp.sum(hidden_grad * mid_normal, axis=0),
                query_gain_part[:, 0],
                key_gain_part[:, 0],
            ]
        ),
        ("seq", "head", "wa"),
    )
    small = small * grad_scale

    def share(start, extent):
        size = extent // shard_count
        return lax.dynamic_slice_in_dim(small, start + plane * size, size, 0)

    return (
        block_out[None],
        grad_tokens[None],
        share(0, model_width),
        joint_total,
        share(2 * model_width, HD),
        share(2 * model_width + HD, HD),
        output_total,
        share(model_width, model_width),
        gate_total,
        up_total,
        down_total,
    )


def per_device(tokens, prenorm, joint_weight, *others):
    team = lax.axis_size("seq") * lax.axis_size("head")
    one_head_each = (
        tokens.shape[0] == 1
        and team == KVH
        and joint_weight.shape[0] == KVH * HD
        and lax.axis_size("wa") == H // KVH + 2
    )
    chosen = per_device_heads if one_head_each else per_device_runs
    return chosen(tokens, prenorm, joint_weight, *others)


def solution(mesh):
    in_specs = (
        P("wa", ("seq", "head"), None),
        P(),
        P("wa", None),
        P(),
        P(),
        P("wa", None),
        P(),
        P("wa", None),
        P("wa", None),
        P("wa", None),
        P("wa", ("seq", "head"), None),
    )
    out_specs = (
        P("wa", ("seq", "head"), None),
        P("wa", ("seq", "head"), None),
        P("wa"),
        P("wa", None),
        P("wa"),
        P("wa"),
        P("wa", None),
        P("wa"),
        P("wa", None),
        P("wa", None),
        P("wa", None),
    )
    return jax.shard_map(
        per_device, mesh=mesh, in_specs=in_specs, out_specs=out_specs, check_vma=False
    )
```

```python
import math

import jax
import jax.numpy as jnp
from jax import lax
from jax.experimental import pallas as pl
from jax.experimental.pallas import tpu as pltpu
from jax.sharding import PartitionSpec as P

H = 16
KVH = 8
HD = 64


EPS = 1e-05
THETA = 1000000.0
BLOCK = 512
TEAM = ("seq", "head")
BF = jnp.bfloat16
F32 = jnp.float32
INTERPRET = False


def inverse_rms(values):
    return lax.rsqrt(jnp.mean(values * values, axis=-1, keepdims=True) + EPS)


def rope_tables(positions, head_depth):
    half_depth = head_depth // 2
    frequency = THETA ** (-(jnp.arange(half_depth).astype(jnp.float32) * 2.0 / head_depth))
    angles = positions.astype(jnp.float32)[:, None] * frequency[None, :]
    return (jnp.cos(angles), jnp.sin(angles))


def rotate(values, cosine, sine):
    half_depth = values.shape[-1] // 2
    front_half = values[..., :half_depth]
    back_half = values[..., half_depth:]
    return jnp.concatenate(
        [front_half * cosine - back_half * sine, back_half * cosine + front_half * sine], axis=-1
    )


def norm_back(grad_normal, normal, inverse):
    return inverse * (grad_normal - normal * jnp.mean(grad_normal * normal, axis=-1, keepdims=True))


def per_device_runs(
    tokens,
    prenorm,
    joint_weight,
    query_gain,
    key_gain,
    output_weight,
    midnorm,
    gate_weight,
    up_weight,
    down_weight,
    cotangent,
):
    seq_local, local_rows, model_width = tokens.shape
    seq_count = lax.axis_size("seq")
    head_count = lax.axis_size("head")
    shard_count = lax.axis_size("wa")
    group_size = H // KVH
    local_heads = KVH // head_count
    run_rows = local_rows * head_count
    block = BLOCK
    query_blocks = run_rows // block
    score_scale = HD ** (-0.5)
    grad_scale = float(shard_count * seq_local * local_rows * seq_count * head_count) ** (-0.5)
    seq_index = lax.axis_index("seq")
    head_index = lax.axis_index("head")
    positions = (seq_index * head_count + head_index) * local_rows + jnp.arange(local_rows)
    run_start = seq_index * run_rows
    cosine, sine = rope_tables(positions, HD)
    cos_query = cosine[None, :, None, None, :]
    sin_query = sine[None, :, None, None, :]
    cos_key = cosine[None, :, None, :]
    sin_key = sine[None, :, None, :]
    query_cols = H * HD
    key_end = query_cols + KVH * HD
    gathered_joint, gathered_output = (
        lax.all_gather(joint_weight, "wa", axis=0, tiled=True),
        lax.all_gather(output_weight, "wa", axis=0, tiled=True),
    )
    resid = tokens.astype(jnp.float32)
    pre_inverse = inverse_rms(resid)
    pre_normal = resid * pre_inverse
    normed = (pre_normal * prenorm).astype(jnp.bfloat16)
    joint = jnp.einsum("std,ed->ste", normed, gathered_joint, preferred_element_type=jnp.float32)
    raw_query = joint[..., :query_cols].reshape(seq_local, local_rows, KVH, group_size, HD)
    raw_key = joint[..., query_cols:key_end].reshape(seq_local, local_rows, KVH, HD)
    values = joint[..., key_end:].reshape(seq_local, local_rows, KVH, HD).astype(jnp.bfloat16)
    query_inverse = inverse_rms(raw_query)
    query_normal = raw_query * query_inverse
    key_inverse = inverse_rms(raw_key)
    key_normal = raw_key * key_inverse
    queries = rotate(query_normal * query_gain, cos_query, sin_query).astype(jnp.bfloat16)
    keys_rot = rotate(key_normal * key_gain, cos_key, sin_key).astype(jnp.bfloat16)
    packed = jnp.concatenate(
        [queries.reshape(seq_local, local_rows, KVH, group_size * HD), keys_rot, values], axis=-1
    )
    by_head = lax.all_to_all(packed, "head", split_axis=2, concat_axis=1, tiled=True)
    head_queries = by_head[..., : group_size * HD].reshape(
        seq_local, run_rows, local_heads, group_size, HD
    )
    key_value = by_head[..., group_size * HD :]
    all_kv = lax.all_gather(key_value, "seq", axis=1, tiled=True)
    all_keys = all_kv[..., :HD]
    all_values = all_kv[..., HD:]

    def masked_scores(query_block, key_block, query_start, key_start):
        scores = (
            jnp.einsum(
                "sqkgd,sjkd->skgqj", query_block, key_block, preferred_element_type=jnp.float32
            )
            * score_scale
        )
        rows_pos = query_start + jnp.arange(block)
        cols_pos = key_start + jnp.arange(block)
        return jnp.where(cols_pos[None, :] <= rows_pos[:, None], scores, -jnp.inf)

    def needed_blocks(query_start):
        return (query_start + block - 1) // block + 1

    stat_shape = (seq_local, local_heads, group_size, block, 1)

    def forward_block(block_no, carry):
        out_buffer, norm_buffer = carry
        row_start = block_no * block
        query_block = lax.dynamic_slice_in_dim(head_queries, row_start, block, 1)
        query_pos = run_start + row_start
        key_count = needed_blocks(query_pos)

        def stats_step(key_no, running):
            row_peak, row_total = running
            col_start = key_no * block
            key_block = lax.dynamic_slice_in_dim(all_keys, col_start, block, 1)
            scores = masked_scores(query_block, key_block, query_pos, col_start)
            new_peak = jnp.maximum(row_peak, jnp.max(scores, axis=-1, keepdims=True))
            row_total = row_total * jnp.exp(row_peak - new_peak) + jnp.sum(
                jnp.exp(scores - new_peak), axis=-1, keepdims=True
            )
            return (new_peak, row_total)

        row_peak, row_total = lax.fori_loop(
            0,
            key_count,
            stats_step,
            (jnp.full(stat_shape, -jnp.inf, jnp.float32), jnp.zeros(stat_shape, jnp.float32)),
        )
        log_norm = row_peak + jnp.log(row_total)

        def value_step(key_no, value_sum):
            col_start = key_no * block
            key_block = lax.dynamic_slice_in_dim(all_keys, col_start, block, 1)
            value_block = lax.dynamic_slice_in_dim(all_values, col_start, block, 1)
            weights = jnp.exp(
                masked_scores(query_block, key_block, query_pos, col_start) - log_norm
            ).astype(jnp.bfloat16)
            return value_sum + jnp.einsum(
                "skgqj,sjkd->sqkgd", weights, value_block, preferred_element_type=jnp.float32
            )

        value_sum = lax.fori_loop(
            0,
            key_count,
            value_step,
            jnp.zeros((seq_local, block, local_heads, group_size, HD), jnp.float32),
        )
        out_buffer = lax.dynamic_update_slice_in_dim(
            out_buffer, value_sum.astype(jnp.bfloat16), row_start, 1
        )
        norm_buffer = lax.dynamic_update_slice_in_dim(norm_buffer, log_norm, row_start, 3)
        return (out_buffer, norm_buffer)

    out_buffer, norm_buffer = lax.fori_loop(
        0,
        query_blocks,
        forward_block,
        (
            jnp.zeros((seq_local, run_rows, local_heads, group_size, HD), jnp.bfloat16),
            jnp.zeros((seq_local, local_heads, group_size, run_rows, 1), jnp.float32),
        ),
    )
    attended_heads = out_buffer.reshape(seq_local, run_rows, local_heads, group_size * HD)
    attn_rows = lax.all_to_all(
        attended_heads, "head", split_axis=1, concat_axis=2, tiled=True
    ).reshape(seq_local, local_rows, H * HD)
    middle = resid + jnp.einsum(
        "ste,de->std", attn_rows, gathered_output, preferred_element_type=jnp.float32
    )
    mid_inverse = inverse_rms(middle)
    mid_normal = middle * mid_inverse
    hidden_in = (mid_normal * midnorm).astype(jnp.bfloat16)
    all_hidden, all_cot = (
        lax.all_gather(hidden_in, "wa", axis=0, tiled=True),
        lax.all_gather(cotangent, "wa", axis=0, tiled=True),
    )
    gate_pre = jnp.einsum(
        "std,fd->stf", all_hidden, gate_weight, preferred_element_type=jnp.float32
    )
    up_pre = jnp.einsum("std,fd->stf", all_hidden, up_weight, preferred_element_type=jnp.float32)
    sigma = jax.nn.sigmoid(gate_pre)
    activ = (gate_pre * sigma * up_pre).astype(jnp.bfloat16)
    ffn_part = jnp.einsum("stf,fd->std", activ, down_weight, preferred_element_type=jnp.float32)
    ffn_out = lax.psum_scatter(ffn_part, "wa", scatter_dimension=0, tiled=True)
    block_out = (middle + ffn_out).astype(jnp.bfloat16)
    act_grad = jnp.einsum("std,fd->stf", all_cot, down_weight, preferred_element_type=jnp.float32)
    gate_back = (act_grad * up_pre * sigma * (1.0 + gate_pre * (1.0 - sigma))).astype(jnp.bfloat16)
    up_back = (act_grad * gate_pre * sigma).astype(jnp.bfloat16)
    grad_down = (
        jnp.einsum("stf,std->fd", activ, all_cot, preferred_element_type=jnp.float32) * grad_scale
    )
    grad_gate = (
        jnp.einsum("stf,std->fd", gate_back, all_hidden, preferred_element_type=jnp.float32)
        * grad_scale
    )
    grad_up = (
        jnp.einsum("stf,std->fd", up_back, all_hidden, preferred_element_type=jnp.float32)
        * grad_scale
    )
    hidden_part = jnp.einsum(
        "stf,fd->std", gate_back, gate_weight, preferred_element_type=jnp.float32
    ) + jnp.einsum("stf,fd->std", up_back, up_weight, preferred_element_type=jnp.float32)
    hidden_grad = lax.psum_scatter(hidden_part, "wa", scatter_dimension=0, tiled=True)
    grad_midnorm = jnp.sum(hidden_grad * mid_normal, axis=(0, 1)) * grad_scale
    middle_grad = cotangent.astype(jnp.float32) + norm_back(
        hidden_grad * midnorm, mid_normal, mid_inverse
    )
    middle_low = middle_grad.astype(jnp.bfloat16)
    grad_output = (
        jnp.einsum("std,ste->de", middle_low, attn_rows, preferred_element_type=jnp.float32)
        * grad_scale
    )
    attended_grad = (
        jnp.einsum("std,de->ste", middle_low, gathered_output, preferred_element_type=jnp.float32)
        .astype(jnp.bfloat16)
        .reshape(seq_local, local_rows, KVH, group_size * HD)
    )
    grad_heads = lax.all_to_all(
        attended_grad, "head", split_axis=2, concat_axis=1, tiled=True
    ).reshape(seq_local, run_rows, local_heads, group_size, HD)
    delta_all = jnp.einsum(
        "sqkgd,sqkgd->skgq", grad_heads, out_buffer, preferred_element_type=jnp.float32
    )[..., None]

    def backward_block(block_no, carry):
        kv_grads, query_grads = carry
        row_start = block_no * block
        query_block = lax.dynamic_slice_in_dim(head_queries, row_start, block, 1)
        grad_block = lax.dynamic_slice_in_dim(grad_heads, row_start, block, 1)
        norm_block = lax.dynamic_slice_in_dim(norm_buffer, row_start, block, 3)
        delta_block = lax.dynamic_slice_in_dim(delta_all, row_start, block, 3)
        query_pos = run_start + row_start

        def key_step(key_no, inner):
            kv_inner, query_sum = inner
            col_start = key_no * block
            key_block = lax.dynamic_slice_in_dim(all_keys, col_start, block, 1)
            value_block = lax.dynamic_slice_in_dim(all_values, col_start, block, 1)
            probs = jnp.exp(
                masked_scores(query_block, key_block, query_pos, col_start) - norm_block
            )
            dot_grad = jnp.einsum(
                "sqkgd,sjkd->skgqj", grad_block, value_block, preferred_element_type=jnp.float32
            )
            score_grad = (probs * (dot_grad - delta_block)).astype(jnp.bfloat16)
            value_term = jnp.einsum(
                "skgqj,sqkgd->sjkd",
                probs.astype(jnp.bfloat16),
                grad_block,
                preferred_element_type=jnp.float32,
            )
            key_term = (
                jnp.einsum(
                    "skgqj,sqkgd->sjkd", score_grad, query_block, preferred_element_type=jnp.float32
                )
                * score_scale
            )
            query_sum = (
                query_sum
                + jnp.einsum(
                    "skgqj,sjkd->sqkgd", score_grad, key_block, preferred_element_type=jnp.float32
                )
                * score_scale
            )
            previous = lax.dynamic_slice_in_dim(kv_inner, col_start, block, 1)
            kv_inner = lax.dynamic_update_slice_in_dim(
                kv_inner, previous + jnp.concatenate([key_term, value_term], axis=-1), col_start, 1
            )
            return (kv_inner, query_sum)

        kv_grads, query_sum = lax.fori_loop(
            0,
            needed_blocks(query_pos),
            key_step,
            (kv_grads, jnp.zeros((seq_local, block, local_heads, group_size, HD), jnp.float32)),
        )
        query_grads = lax.dynamic_update_slice_in_dim(
            query_grads, query_sum.astype(jnp.bfloat16), row_start, 1
        )
        return (kv_grads, query_grads)

    kv_grads, query_grads = lax.fori_loop(
        0,
        query_blocks,
        backward_block,
        (
            jnp.zeros((seq_local, seq_count * run_rows, local_heads, 2 * HD), jnp.float32),
            jnp.zeros((seq_local, run_rows, local_heads, group_size, HD), jnp.bfloat16),
        ),
    )
    kv_sums = lax.psum_scatter(kv_grads, "seq", scatter_dimension=1, tiled=True).astype(
        jnp.bfloat16
    )
    back_pack = jnp.concatenate(
        [query_grads.reshape(seq_local, run_rows, local_heads, group_size * HD), kv_sums], axis=-1
    )
    back_tokens = lax.all_to_all(back_pack, "head", split_axis=1, concat_axis=2, tiled=True)
    query_wide = (
        back_tokens[..., : group_size * HD]
        .reshape(seq_local, local_rows, KVH, group_size, HD)
        .astype(jnp.float32)
    )
    key_wide = back_tokens[..., group_size * HD : group_size * HD + HD].astype(jnp.float32)
    value_back = back_tokens[..., group_size * HD + HD :]
    query_scaled = rotate(query_wide, cos_query, -sin_query)
    grad_query_all = jnp.sum(query_scaled * query_normal, axis=(0, 1, 2, 3)) * grad_scale
    query_raw = norm_back(query_scaled * query_gain, query_normal, query_inverse)
    key_scaled = rotate(key_wide, cos_key, -sin_key)
    grad_key_all = jnp.sum(key_scaled * key_normal, axis=(0, 1, 2)) * grad_scale
    key_raw = norm_back(key_scaled * key_gain, key_normal, key_inverse)
    joint_back = jnp.concatenate(
        [
            query_raw.reshape(seq_local, local_rows, H * HD).astype(jnp.bfloat16),
            key_raw.reshape(seq_local, local_rows, KVH * HD).astype(jnp.bfloat16),
            value_back.reshape(seq_local, local_rows, KVH * HD),
        ],
        axis=-1,
    )
    normed_grad = jnp.einsum(
        "ste,ed->std", joint_back, gathered_joint, preferred_element_type=jnp.float32
    )
    grad_joint_all = (
        jnp.einsum("ste,std->ed", joint_back, normed, preferred_element_type=jnp.float32)
        * grad_scale
    )
    grad_prenorm_all = jnp.sum(normed_grad * pre_normal, axis=(0, 1)) * grad_scale
    grad_tokens = middle_grad + norm_back(normed_grad * prenorm, pre_normal, pre_inverse)
    joint_share, output_share, prenorm_share, query_share, key_share, midnorm_share = (
        lax.psum_scatter(grad_joint_all, "wa", scatter_dimension=0, tiled=True),
        lax.psum_scatter(grad_output, "wa", scatter_dimension=0, tiled=True),
        lax.psum_scatter(grad_prenorm_all, "wa", scatter_dimension=0, tiled=True),
        lax.psum_scatter(grad_query_all, "wa", scatter_dimension=0, tiled=True),
        lax.psum_scatter(grad_key_all, "wa", scatter_dimension=0, tiled=True),
        lax.psum_scatter(grad_midnorm, "wa", scatter_dimension=0, tiled=True),
    )
    (
        joint_total,
        output_total,
        prenorm_total,
        query_total,
        key_total,
        midnorm_total,
        gate_total,
        up_total,
        down_total,
    ) = lax.psum(
        (
            joint_share,
            output_share,
            prenorm_share,
            query_share,
            key_share,
            midnorm_share,
            grad_gate,
            grad_up,
            grad_down,
        ),
        ("seq", "head"),
    )
    return (
        block_out,
        grad_tokens,
        prenorm_total,
        joint_total,
        query_total,
        key_total,
        output_total,
        midnorm_total,
        gate_total,
        up_total,
        down_total,
    )


def split(values, axis):
    return jnp.split(values, 2, axis=axis)


def rotate_rows(values, cosine, sine):
    front_half, back_half = split(values, 0)
    return jnp.concatenate(
        [front_half * cosine - back_half * sine, back_half * cosine + front_half * sine], axis=0
    )


def inverse_rms_rows(values):
    return lax.rsqrt(jnp.mean(values * values, axis=0, keepdims=True) + EPS)


def norm_back_rows(grad_normal, normal, inverse):
    return inverse * (grad_normal - normal * jnp.mean(grad_normal * normal, axis=0, keepdims=True))


def turned(values):
    return jnp.transpose(values.astype(F32)).astype(BF)


def dot(left, right):
    return jnp.dot(left, right, preferred_element_type=F32)


def attend_kernel(
    table_ref,
    *refs,
):
    outputs_from = len(refs) - 12
    *tile_refs, cos_ref, sin_ref, query_gain_ref, key_gain_ref = refs[:outputs_from]
    out_ref, norm_ref, query_ref, key_ref, key_rows_ref, value_ref = refs[outputs_from:][:6]
    joint_out_ref, weight_ref, key_s, value_rows_s, score_s, joint_s = refs[outputs_from:][6:]
    step = pl.program_id(0)
    place = table_ref[0]
    blocks, _, rows = joint_s.shape
    tile_refs, slot_refs = tile_refs[:blocks], tile_refs[blocks:]
    heads = query_ref.shape[2] // rows

    @pl.when(step == 0)
    def project():
        start = pl.multiple_of((place % heads) * HD, HD)
        for slot, slot_ref in enumerate(slot_refs):

            @pl.when(table_ref[1] == slot)
            def queries():
                weight_ref[: heads * HD] = slot_ref[...]

            for part in range(2):

                @pl.when(table_ref[2 + part] == slot)
                def keys():
                    weight_ref[(heads + part) * HD : (heads + part + 1) * HD] = slot_ref[
                        pl.ds(start, HD)
                    ]

        for mask, tile_ref in enumerate(tile_refs):
            joint_s[mask ^ place] = lax.dot_general(
                weight_ref[...],
                tile_ref[...],
                (((1,), (1,)), ((), ())),
                preferred_element_type=F32,
            )

    joint_out_ref[0] = joint_s[step]
    cosine, sine = cos_ref[0], sin_ref[0]
    query_gain, key_gain = query_gain_ref[...], key_gain_ref[...]
    raw = joint_s[step]
    parts = []
    for head in range(heads):
        raw_query = raw[head * HD : (head + 1) * HD]
        normal = raw_query * inverse_rms_rows(raw_query)
        parts.append(rotate_rows(normal * query_gain, cosine, sine).astype(BF))
    scale = jnp.asarray(HD ** (-0.5), BF)
    queries = jnp.concatenate(parts, axis=1) * scale
    raw_key = raw[heads * HD : (heads + 1) * HD]
    key_normal = raw_key * inverse_rms_rows(raw_key)
    keys_f32 = rotate_rows(key_normal * key_gain, cosine, sine)
    values_f32 = raw[(heads + 1) * HD :]
    keys = jnp.transpose(keys_f32).astype(BF)
    value_rows = values_f32.astype(BF)
    query_ref[0] = queries
    key_ref[0] = keys
    key_rows_ref[0] = keys_f32.astype(BF)
    value_ref[0] = jnp.transpose(values_f32).astype(BF)
    key_s[step] = keys
    value_rows_s[step] = value_rows
    lanes = heads * rows

    def fold(scores, reducer):
        return reducer(scores.reshape(rows // 8, 8, lanes), axis=0)

    key_pos = lax.broadcasted_iota(jnp.int32, (rows, rows), 0)
    query_pos = lax.broadcasted_iota(jnp.int32, (rows, rows), 1)
    allowed = jnp.concatenate([key_pos <= query_pos] * heads, axis=1)
    own = jnp.where(allowed, dot(keys, queries), -jnp.inf)
    score_s[step] = own

    def peak_step(block_no, peak):
        scores = dot(key_s[block_no], queries)
        score_s[block_no] = scores
        return jnp.maximum(peak, fold(scores, jnp.max))

    peak = lax.fori_loop(0, step, peak_step, fold(own, jnp.max))
    peak = jnp.max(peak, axis=0, keepdims=True)

    def sum_step(block_no, carry):
        total, value_sum = carry
        weights = jnp.exp(score_s[block_no] - peak)
        total = total + fold(weights, jnp.sum)
        value_sum = value_sum + dot(value_rows_s[block_no], weights.astype(BF))
        return total, value_sum

    total, value_sum = lax.fori_loop(
        0, step + 1, sum_step, (jnp.zeros((8, lanes), F32), jnp.zeros((HD, lanes), F32))
    )
    total = jnp.sum(total, axis=0, keepdims=True)
    attended = (value_sum / total).astype(BF)
    norm_ref[0] = peak + jnp.log(total)
    for head in range(heads):
        out_ref[0, head * HD : (head + 1) * HD] = attended[:, head * rows : (head + 1) * rows]


def attend(table, tiles, slots, cosine, sine, query_gain, key_gain):
    blocks = len(tiles)
    rows, model_width = tiles[0].shape
    heads = slots[0].shape[0] // HD
    width = (heads + 2) * HD
    lanes = heads * rows
    whole = lambda shape: pl.BlockSpec(shape, lambda i, p: (0,) * len(shape))
    one = lambda *shape: pl.BlockSpec((1,) + shape, lambda i, p: (i,) + (0,) * len(shape))
    struct = jax.ShapeDtypeStruct
    return pl.pallas_call(
        attend_kernel,
        grid_spec=pltpu.PrefetchScalarGridSpec(
            num_scalar_prefetch=1,
            grid=(blocks,),
            in_specs=[whole(array.shape) for array in (*tiles, *slots)]
            + [one(HD // 2, rows), one(HD // 2, rows), whole((HD, 1)), whole((HD, 1))],
            out_specs=[
                pl.BlockSpec((1, heads * HD, rows), lambda i, p: (i ^ p[0], 0, 0)),
                one(1, lanes),
                one(HD, lanes),
                one(rows, HD),
                one(HD, rows),
                one(rows, HD),
                one(width, rows),
                whole((width, model_width)),
            ],
            scratch_shapes=[
                pltpu.VMEM((blocks, rows, HD), BF),
                pltpu.VMEM((blocks, HD, rows), BF),
                pltpu.VMEM((blocks, rows, lanes), F32),
                pltpu.VMEM((blocks, width, rows), F32),
            ],
        ),
        out_shape=[
            struct((blocks, heads * HD, rows), BF),
            struct((blocks, 1, lanes), F32),
            struct((blocks, HD, lanes), BF),
            struct((blocks, rows, HD), BF),
            struct((blocks, HD, rows), BF),
            struct((blocks, rows, HD), BF),
            struct((blocks, width, rows), F32),
            struct((width, model_width), BF),
        ],
        interpret=INTERPRET,
        name="attend",
    )(table, *tiles, *slots, cosine, sine, query_gain, key_gain)


def attend_back_kernel(
    place_ref,
    *refs,
):
    blocks = (len(refs) - 19) // 2
    grad_refs, tile_refs, refs = refs[:blocks], refs[blocks : 2 * blocks], refs[2 * blocks :]
    out_ref, norm_ref, query_ref, key_ref, key_rows_ref, value_ref, joint_ref = refs[:7]
    cos_ref, sin_ref, query_gain_ref, key_gain_ref, back_ref, head_part_ref = refs[7:13]
    query_gain_grad_ref, key_gain_grad_ref, key_acc, value_acc, gain_acc, grad_s = refs[13:]
    step = pl.program_id(0)
    place = place_ref[0]
    rows = grad_s.shape[2]
    heads = query_ref.shape[2] // rows
    lanes = heads * rows

    @pl.when(step == 0)
    def clear():
        key_acc[...] = jnp.zeros(key_acc.shape, F32)
        value_acc[...] = jnp.zeros(value_acc.shape, F32)
        gain_acc[...] = jnp.zeros(gain_acc.shape, F32)
        for mask, grad_ref in enumerate(grad_refs):
            grad_s[mask ^ place] = grad_ref[...]

    def side_by_side(ref, block_no):
        return jnp.concatenate(
            [ref[block_no, h * HD : (h + 1) * HD] for h in range(heads)], axis=1
        )

    grads = side_by_side(grad_s, step)
    delta = jnp.sum(grads.astype(F32) * side_by_side(out_ref, 0).astype(F32), axis=0, keepdims=True)
    norm = norm_ref[0]
    queries = query_ref[0]
    query_cols = turned(queries)
    grad_cols = turned(grads)
    key_pos = lax.broadcasted_iota(jnp.int32, (rows, rows), 0)
    query_pos = lax.broadcasted_iota(jnp.int32, (rows, rows), 1)
    allowed = jnp.concatenate([key_pos <= query_pos] * heads, axis=1)

    def block_step(block_no, query_sum, mask):
        probs = jnp.exp(dot(key_ref[block_no], queries) - norm)
        if mask:
            probs = jnp.where(allowed, probs, 0.0)
        score_grad = (probs * (dot(value_ref[block_no], grads) - delta)).astype(BF)
        value_acc[block_no] += dot(probs.astype(BF), grad_cols)
        key_acc[block_no] += dot(score_grad, query_cols)
        return query_sum + dot(key_rows_ref[block_no], score_grad)

    query_sum = block_step(step, jnp.zeros((HD, lanes), F32), True)
    query_sum = lax.fori_loop(0, step, lambda b, s: block_step(b, s, False), query_sum)
    query_grad = (query_sum * HD ** (-0.5)).astype(BF).astype(F32)
    cosine, sine = cos_ref[step], sin_ref[step]
    query_gain = query_gain_ref[...]
    for head in range(heads):
        raw = joint_ref[step, head * HD : (head + 1) * HD]
        inverse = inverse_rms_rows(raw)
        normal = raw * inverse
        scaled = rotate_rows(query_grad[:, head * rows : (head + 1) * rows], cosine, -sine)
        gain_acc[0] += scaled * normal
        back_ref[step ^ place, head * HD : (head + 1) * HD] = norm_back_rows(
            scaled * query_gain, normal, inverse
        ).astype(BF)

    @pl.when(step == pl.num_programs(0) - 1)
    def finish():
        key_gain = key_gain_ref[...]

        def finish_block(block_no, carry):
            raw = joint_ref[block_no, heads * HD : (heads + 1) * HD]
            inverse = inverse_rms_rows(raw)
            normal = raw * inverse
            key_grad = jnp.transpose(key_acc[block_no]).astype(BF).astype(F32)
            scaled = rotate_rows(key_grad, cos_ref[block_no], -sin_ref[block_no])
            gain_acc[1] += scaled * normal
            back_ref[block_no ^ place, heads * HD : (heads + 1) * HD] = norm_back_rows(
                scaled * key_gain, normal, inverse
            ).astype(BF)
            back_ref[block_no ^ place, (heads + 1) * HD :] = jnp.transpose(value_acc[block_no]).astype(BF)
            return carry

        lax.fori_loop(0, pl.num_programs(0), finish_block, 0)
        ones = jnp.ones((8, rows), F32)
        for gain_no, gain_ref in enumerate((query_gain_grad_ref, key_gain_grad_ref)):
            gain_ref[...] = lax.dot_general(
                ones,
                gain_acc[gain_no],
                (((1,), (1,)), ((), ())),
                precision=lax.Precision.HIGHEST,
                preferred_element_type=F32,
            )
        head_part = dot(back_ref[0], tile_refs[0][...])
        for mask in range(1, blocks):
            head_part = head_part + dot(back_ref[mask], tile_refs[mask][...])
        head_part_ref[...] = head_part.astype(BF)


def attend_back(
    place, grads, tiles, attended, saved, joint_rows, cosine, sine, query_gain, key_gain
):
    norm, queries, keys, key_rows, values = saved
    blocks, width, rows = joint_rows.shape
    heads = width // HD - 2
    lanes = heads * rows
    whole = lambda shape: pl.BlockSpec(shape, lambda i, p: (0,) * len(shape))
    one = lambda *shape: pl.BlockSpec((1,) + shape, lambda i, p: (i,) + (0,) * len(shape))
    struct = jax.ShapeDtypeStruct
    outs = [
        struct(joint_rows.shape, BF),
        struct((width, tiles[0].shape[1]), BF),
        struct((8, HD), F32),
        struct((8, HD), F32),
    ]
    return pl.pallas_call(
        attend_back_kernel,
        grid_spec=pltpu.PrefetchScalarGridSpec(
            num_scalar_prefetch=1,
            grid=(blocks,),
            in_specs=[whole(array.shape) for array in (*grads, *tiles)]
            + [
                pl.BlockSpec((1, heads * HD, rows), lambda i, p: (i ^ p[0], 0, 0)),
                one(1, lanes),
                one(HD, lanes),
            ]
            + [whole(array.shape) for array in (keys, key_rows, values, joint_rows)]
            + [whole(array.shape) for array in (cosine, sine, query_gain, key_gain)],
            out_specs=[whole(out.shape) for out in outs],
            scratch_shapes=[
                pltpu.VMEM((blocks, rows, HD), F32),
                pltpu.VMEM((blocks, rows, HD), F32),
                pltpu.VMEM((2, HD, rows), F32),
                pltpu.VMEM((blocks, heads * HD, rows), BF),
            ],
        ),
        out_shape=outs,
        interpret=INTERPRET,
        name="attend_back",
    )(
        place, *grads, *tiles, attended, norm, queries, keys, key_rows, values,
        joint_rows, cosine, sine, query_gain, key_gain,
    )


def middle_kernel(place_ref, *refs):
    *tile_refs, weight_ref, token_ref, gain_ref, middle_ref, hidden_ref, ordered_ref = refs
    columns = []
    for mask, tile_ref in enumerate(tile_refs):
        tile = tile_ref[...]
        ordered_ref[mask ^ place_ref[0]] = tile
        columns.append(turned(tile))
    middle = token_ref[...].astype(F32) + lax.dot_general(
        jnp.concatenate(columns, axis=1),
        weight_ref[...],
        (((1,), (1,)), ((), ())),
        preferred_element_type=F32,
    )
    middle_ref[...] = middle
    hidden_ref[...] = (middle * inverse_rms(middle) * gain_ref[...]).astype(BF)


def project_middle(place, tiles, weight, tokens, gain):
    struct = jax.ShapeDtypeStruct
    whole = lambda shape: pl.BlockSpec(shape, lambda i, p: (0,) * len(shape))
    arrays = (*tiles, weight, tokens, gain)
    outs = [
        struct(tokens.shape, F32),
        struct(tokens.shape, BF),
        struct((len(tiles),) + tiles[0].shape, BF),
    ]
    return pl.pallas_call(
        middle_kernel,
        grid_spec=pltpu.PrefetchScalarGridSpec(
            num_scalar_prefetch=1,
            grid=(1,),
            in_specs=[whole(array.shape) for array in arrays],
            out_specs=[whole(out.shape) for out in outs],
        ),
        out_shape=outs,
        interpret=INTERPRET,
        name="project_middle",
    )(place, *arrays)


def place_output_kernel(table_ref, *refs):
    *piece_refs, out_ref = refs
    place = table_ref[0]
    shards, team, rows, width = out_ref.shape
    group = width // team
    for mask, piece_ref in enumerate(piece_refs):
        for slot in range(shards):
            piece = piece_ref[slot * rows : (slot + 1) * rows]
            for column in range(team):
                start = pl.multiple_of((column ^ place) * group, group)
                out_ref[table_ref[1 + slot], mask ^ place, :, pl.ds(start, group)] = piece[
                    :, column * group : (column + 1) * group
                ]


def place_output(table, tiles, shards):
    rows, width = tiles[0].shape
    team = len(tiles)
    rows //= shards
    return pl.pallas_call(
        place_output_kernel,
        grid_spec=pltpu.PrefetchScalarGridSpec(
            num_scalar_prefetch=1,
            grid=(1,),
            in_specs=[pl.BlockSpec(tile.shape, lambda i, t: (0, 0)) for tile in tiles],
            out_specs=pl.BlockSpec((shards, team, rows, width), lambda i, t: (0, 0, 0, 0)),
        ),
        out_shape=jax.ShapeDtypeStruct((shards, team, rows, width), BF),
        interpret=INTERPRET,
        name="place_output",
    )(table, *tiles)


def widen_kernel(table_ref, *refs, index, scale):
    *piece_refs, out_ref = refs
    quarters = len(piece_refs) // 2
    half = piece_refs[0].shape[1]
    first = table_ref[0] == 0
    block_no = index * pl.num_programs(0) + pl.program_id(0)
    for number in range(quarters):

        @pl.when(block_no // table_ref[1] == table_ref[2 + number])
        def store():
            own = piece_refs[number][...].astype(F32) * scale
            other = piece_refs[quarters + number][...].astype(F32) * scale
            out_ref[:, :half] = jnp.where(first, own, other)
            out_ref[:, half:] = jnp.where(first, other, own)


def widen(table, pieces, index, count, scale):
    quarters = len(pieces) // 2
    rows, half = pieces[0].shape
    block = math.gcd(rows, rows * quarters // count)
    steps = rows * quarters // count // block
    per_piece = rows // block

    def piece_spec(number):
        def index_map(i, t):
            return (jnp.clip(index * steps + i - per_piece * t[2 + number], 0, per_piece - 1), 0)

        return pl.BlockSpec((block, half), index_map)

    return pl.pallas_call(
        lambda *refs: widen_kernel(*refs, index=index, scale=scale),
        grid_spec=pltpu.PrefetchScalarGridSpec(
            num_scalar_prefetch=1,
            grid=(steps,),
            in_specs=[piece_spec(number % quarters) for number in range(2 * quarters)],
            out_specs=pl.BlockSpec((block, 2 * half), lambda i, t: (i, 0)),
        ),
        out_shape=jax.ShapeDtypeStruct((steps * block, 2 * half), F32),
        interpret=INTERPRET,
        name="widen",
    )(table, *pieces)


def last_rows_kernel(table_ref, *refs, scale, query_rows, query_shards):
    *tile_refs, joint_ref, output_ref = refs
    place, plane = table_ref[0], table_ref[1]
    team = len(tile_refs)
    per_shard = team // query_shards
    rows = output_ref.shape[0] // team
    for mask, tile_ref in enumerate(tile_refs):
        source = place ^ mask
        start = pl.multiple_of(table_ref[2 + mask] * rows, rows)
        output_ref[pl.ds(start, rows)] = tile_ref[query_rows:].astype(F32) * scale
        slot = source - plane * per_shard

        @pl.when(jnp.logical_and(slot >= 0, slot < per_shard))
        def queries():
            joint_ref[pl.ds(pl.multiple_of(slot * query_rows, query_rows), query_rows)] = (
                tile_ref[:query_rows].astype(F32) * scale
            )

        for part in range(2):

            @pl.when(plane == query_shards + part)
            def keys():
                joint_ref[pl.ds(pl.multiple_of(source * HD, HD), HD)] = (
                    tile_ref[part * HD : (part + 1) * HD].astype(F32) * scale
                )


def last_rows(table, tiles, joint_shape, output_shape, scale, query_rows, query_shards):
    struct = jax.ShapeDtypeStruct
    return pl.pallas_call(
        lambda *refs: last_rows_kernel(
            *refs, scale=scale, query_rows=query_rows, query_shards=query_shards
        ),
        grid_spec=pltpu.PrefetchScalarGridSpec(
            num_scalar_prefetch=1,
            grid=(1,),
            in_specs=[pl.BlockSpec(tile.shape, lambda i, t: (0, 0)) for tile in tiles],
            out_specs=[
                pl.BlockSpec(joint_shape, lambda i, t: (0, 0)),
                pl.BlockSpec(output_shape, lambda i, t: (0, 0)),
            ],
        ),
        out_shape=[struct(joint_shape, F32), struct(output_shape, F32)],
        interpret=INTERPRET,
        name="last_rows",
    )(table, *tiles)


def per_device_heads(
    tokens,
    prenorm,
    joint_weight,
    query_gain,
    key_gain,
    output_weight,
    midnorm,
    gate_weight,
    up_weight,
    down_weight,
    cotangent,
):
    _, local_rows, model_width = tokens.shape
    head_count = lax.axis_size("head")
    shard_count = lax.axis_size("wa")
    team = lax.axis_size("seq") * head_count
    group_size = H // KVH
    head_width = (group_size + 2) * HD
    grad_scale = float(shard_count * local_rows * team) ** (-0.5)
    place = lax.axis_index(TEAM)
    plane = lax.axis_index("wa")
    near = head_count
    far = [1 << b for b in range(team.bit_length() - 1) if 1 << b != near]
    both = far[0] ^ far[1]

    def swap(values, mask):
        return lax.ppermute(values, TEAM, [(i, i ^ mask) for i in range(team)])

    def bit(mask):
        return (place // mask) % 2

    def after(values, *others):
        return lax.optimization_barrier((values,) + others)[0]

    order = [0] + list(range(1, shard_count, 2)) + list(range(2, shard_count, 2))[::-1]
    ring_pairs = [(order[i], order[(i + 1) % shard_count]) for i in range(shard_count)]

    def pick(table, index):
        return sum(jnp.where(index == k, entry, 0) for k, entry in enumerate(table))

    ring_place = pick([order.index(k) for k in range(shard_count)], plane)

    def ring(values):
        return lax.ppermute(values, "wa", ring_pairs)

    def ring_back(values):
        return lax.ppermute(values, "wa", [(b, a) for a, b in ring_pairs])

    def owner(slot):
        return pick(order, (ring_place - slot) % shard_count)

    def slot_of(shard):
        return (ring_place - pick([order.index(k) for k in range(shard_count)], shard)) % shard_count

    def ring_gather(values):
        slots = [values]
        for _ in range(shard_count - 1):
            slots.append(ring(slots[-1]))
        return slots

    def ring_gather_both(values):
        slots = {0: values}
        for step in range(1, shard_count):
            if step <= shard_count // 2:
                slots[step] = ring(slots[step - 1])
        for step in range(shard_count - 1, shard_count // 2, -1):
            slots[step] = ring_back(slots[(step + 1) % shard_count])
        return [slots[step] for step in range(shard_count)]

    def ring_reduce(slots):
        middle_slot = shard_count // 2
        backward = slots[middle_slot].astype(BF)
        for slot in range(middle_slot - 1, 0, -1):
            backward = (ring_back(backward).astype(F32) + slots[slot]).astype(BF)
        total = slots[0] + ring_back(backward).astype(F32)
        if middle_slot + 1 < shard_count:
            forward = slots[middle_slot + 1].astype(BF)
            for slot in range(middle_slot + 2, shard_count):
                forward = (ring(forward).astype(F32) + slots[slot]).astype(BF)
            total = total + ring(forward).astype(F32)
        return total

    def with_near(tiles):
        for mask in (0, far[0], far[1], both):
            tiles[mask ^ near] = swap(tiles[mask], near)
        return [tiles[mask] for mask in range(team)]

    def team_gather(tile):
        tiles = {mask: swap(tile, mask) for mask in (far[0], far[1], both)}
        tiles[0] = tile
        return with_near(tiles)

    def exchange(tiles):
        return [tiles[0]] + [swap(tiles[mask], mask) for mask in range(1, team)]

    def quarter(mask):
        source = place ^ mask
        return (source // far[0]) % 2 * 2 + (source // far[1]) % 2

    def add_quarters(values):
        rows = values.shape[-2] // 4
        axis = values.ndim - 2
        parts = {
            mask: lax.dynamic_slice_in_dim(values, quarter(mask) * rows, rows, axis)
            for mask in (0, far[0], far[1], both)
        }
        total = parts[0].astype(F32)
        for mask in (both, far[0], far[1]):
            total = total + swap(parts[mask], mask).astype(F32)
        return total.astype(BF)

    place_table = place.reshape(1)
    positions = jnp.arange(team * local_rows).astype(F32)
    half_depth = HD // 2
    frequency = THETA ** (-(jnp.arange(half_depth).astype(F32) * 2.0 / HD))
    angles = positions.reshape(team, 1, local_rows) * frequency[None, :, None]
    cosine, sine = jnp.cos(angles), jnp.sin(angles)
    query_gain_col, key_gain_col = query_gain[:, None], key_gain[:, None]

    resid = tokens[0].astype(F32)
    pre_inverse = inverse_rms(resid)
    pre_normal = resid * pre_inverse
    normed = (pre_normal * prenorm).astype(BF)
    normed_tiles = team_gather(normed)

    shard_rows = joint_weight.shape[0]
    query_rows = group_size * HD
    query_shards = KVH * query_rows // shard_rows
    query_shard = place * query_rows // shard_rows
    query_offset = place * query_rows % shard_rows
    key_offset = place // group_size * query_rows
    piece = lax.dynamic_slice_in_dim(
        joint_weight, jnp.where(plane < query_shards, query_offset, key_offset), query_rows, 0
    )
    weight_slots = ring_gather_both(piece)
    head_table = jnp.stack(
        [place, slot_of(query_shard), slot_of(query_shards), slot_of(query_shards + 1)]
    )

    piece_rows = output_weight.shape[0] // team
    output_piece = lax.dynamic_slice_in_dim(output_weight, place * piece_rows, piece_rows, 0)
    output_slots = jnp.concatenate(ring_gather_both(output_piece), axis=0)
    cot_slots = ring_gather_both(after(cotangent[0], *weight_slots))
    output_tiles = team_gather(after(output_slots, normed_tiles[both]))

    attended, *saved, joint_rows, head_weight = attend(
        head_table, normed_tiles, weight_slots, cosine, sine, query_gain_col, key_gain_col
    )
    attn_tiles = exchange(after(attended, cot_slots[1], cot_slots[shard_count - 1]))
    owners = jnp.stack([place] + [owner(slot) for slot in range(shard_count)])
    whole_output = place_output(owners, output_tiles, shard_count).reshape(-1, H * HD)
    middle, hidden_in, attn_ordered = project_middle(
        place_table, attn_tiles, whole_output, tokens[0], midnorm[None]
    )
    attn_ordered = attn_ordered.reshape(H * HD, local_rows)
    mid_inverse = inverse_rms(middle)
    mid_normal = middle * mid_inverse
    hidden_slots = ring_gather(hidden_in)
    joint_tiles = team_gather(after(head_weight, hidden_in))

    acts, gate_backs, up_backs, out_parts, hidden_parts = [], [], [], [], []
    for hidden, cot in zip(hidden_slots, cot_slots):
        gate_pre = jnp.einsum("td,fd->tf", hidden, gate_weight, preferred_element_type=F32)
        up_pre = jnp.einsum("td,fd->tf", hidden, up_weight, preferred_element_type=F32)
        act_grad = jnp.einsum("td,fd->tf", cot, down_weight, preferred_element_type=F32)
        sigma = jax.nn.sigmoid(gate_pre)
        acts.append((gate_pre * sigma * up_pre).astype(BF))
        gate_backs.append(
            (act_grad * up_pre * sigma * (1.0 + gate_pre * (1.0 - sigma))).astype(BF)
        )
        up_backs.append((act_grad * gate_pre * sigma).astype(BF))
        hidden_parts.append(dot(gate_backs[-1], gate_weight) + dot(up_backs[-1], up_weight))
        out_parts.append(dot(acts[-1], down_weight))
    hidden_grad = ring_reduce(hidden_parts)

    all_hidden = jnp.concatenate(hidden_slots, axis=0)
    all_cot = jnp.concatenate(cot_slots, axis=0)
    back_list = [jnp.concatenate(parts, axis=0) for parts in (acts, gate_backs, up_backs)]
    half_width = model_width // 2

    def weight_grads(half):
        columns = [
            lax.dynamic_slice_in_dim(inputs, half * half_width, half_width, 1)
            for inputs in (all_cot, all_hidden)
        ]
        return jnp.concatenate(
            [
                jnp.einsum("tf,td->fd", backs, columns[min(k, 1)], preferred_element_type=F32)
                for k, backs in enumerate(back_list)
            ],
            axis=0,
        )

    sent_grads = swap(weight_grads(1 - bit(near)).astype(BF), near)
    ffn_grads = (weight_grads(bit(near)) + sent_grads.astype(F32)).astype(BF)

    cot = cotangent[0].astype(F32)
    middle_grad = cot + norm_back(hidden_grad * midnorm, mid_normal, mid_inverse)
    middle_low = middle_grad.astype(BF)
    attended_grad = jnp.einsum(
        "td,de->et", middle_low, whole_output, preferred_element_type=F32
    ).astype(BF)
    attended_grad = attended_grad.reshape(team, query_rows, local_rows)
    head_grads = exchange(attended_grad)

    ffn_grads = after(ffn_grads, attended_grad)
    with jax.named_scope("ffn_far"):
        ffn_grads = add_quarters(ffn_grads)

    low_blocks = middle_low.reshape(local_rows, shard_count, 2, -1)

    def output_grads(half):
        rows = lax.dynamic_index_in_dim(low_blocks, half, 2, keepdims=False)
        return jnp.einsum("tpd,et->pde", rows, attn_ordered, preferred_element_type=F32)

    sent_output = swap(output_grads(1 - bit(near)).astype(BF), near)
    output_part = (output_grads(bit(near)) + sent_output.astype(F32)).astype(BF)
    with jax.named_scope("output_far"):
        output_part = add_quarters(output_part)

    back_rows, head_part, query_gain_part, key_gain_part = attend_back(
        place_table, head_grads, normed_tiles, attended, saved, joint_rows, cosine, sine,
        query_gain_col, key_gain_col,
    )
    back_tiles = [back_rows[mask] for mask in range(team)]

    shares = [
        jnp.concatenate(
            [
                lax.dynamic_slice_in_dim(
                    head_part, jnp.where(owner(slot) < query_shards, 0, query_rows), query_rows, 0
                ),
                lax.dynamic_index_in_dim(output_part, owner(slot), 0, keepdims=False),
            ],
            axis=0,
        )
        for slot in range(shard_count)
    ]
    share_total = ring_reduce(shares).astype(BF)

    token_back = jnp.concatenate(exchange(back_tiles), axis=0)
    whole_joint = jnp.concatenate(joint_tiles, axis=0)
    normed_grad = jnp.einsum("et,ed->td", token_back, whole_joint, preferred_element_type=F32)
    grad_tokens = middle_grad + norm_back(normed_grad * prenorm, pre_normal, pre_inverse)

    spread = [ffn_grads] + [swap(ffn_grads, mask) for mask in (both, far[0], far[1])]
    spread = spread + [swap(piece, near) for piece in spread]
    blocks = spread[0].shape[0] * 4 // len(back_list)
    widen_table = jnp.stack(
        [bit(near), jnp.int32(spread[0].shape[0] // math.gcd(spread[0].shape[0], blocks))]
        + [quarter(mask) for mask in (0, both, far[0], far[1])]
    )
    down_total, gate_total, up_total = [
        widen(widen_table, spread, k, len(back_list), grad_scale) for k in range(len(back_list))
    ]

    out_parts[shard_count // 2] = after(out_parts[shard_count // 2], hidden_grad)
    out_parts[shard_count // 2 + 1] = after(out_parts[shard_count // 2 + 1], hidden_grad)
    block_out = (middle + ring_reduce(out_parts)).astype(BF)

    def part_of(mask):
        source = place ^ mask
        index = source * 0
        for part_mask in [near] + far:
            index = index * 2 + (source // part_mask) % 2
        return index

    table = jnp.stack([place, plane] + [part_of(mask) for mask in range(team)])
    joint_total, output_total = last_rows(
        table,
        team_gather(share_total),
        joint_weight.shape,
        output_weight.shape,
        grad_scale,
        query_rows,
        query_shards,
    )

    small = jnp.concatenate(
        [
            jnp.sum(normed_grad * pre_normal, axis=0),
            jnp.sum(hidden_grad * mid_normal, axis=0),
            query_gain_part[0],
            key_gain_part[0],
        ]
    )
    for mask in [near] + far:
        small = small + swap(small, mask)
    gathered = ring_gather_both(small)
    small = sum(gathered[1:], gathered[0]) * grad_scale

    def share(start, extent):
        size = extent // shard_count
        return lax.dynamic_slice_in_dim(small, start + plane * size, size, 0)

    return (
        block_out[None],
        grad_tokens[None],
        share(0, model_width),
        joint_total,
        share(2 * model_width, HD),
        share(2 * model_width + HD, HD),
        output_total,
        share(model_width, model_width),
        gate_total,
        up_total,
        down_total,
    )


def per_device(tokens, prenorm, joint_weight, *others):
    team = lax.axis_size("seq") * lax.axis_size("head")
    one_head_each = (
        tokens.shape[0] == 1
        and team == KVH
        and joint_weight.shape[0] == KVH * HD
        and lax.axis_size("wa") == H // KVH + 2
    )
    chosen = per_device_heads if one_head_each else per_device_runs
    return chosen(tokens, prenorm, joint_weight, *others)


def solution(mesh):
    in_specs = (
        P("wa", ("seq", "head"), None),
        P(),
        P("wa", None),
        P(),
        P(),
        P("wa", None),
        P(),
        P("wa", None),
        P("wa", None),
        P("wa", None),
        P("wa", ("seq", "head"), None),
    )
    out_specs = (
        P("wa", ("seq", "head"), None),
        P("wa", ("seq", "head"), None),
        P("wa"),
        P("wa", None),
        P("wa"),
        P("wa"),
        P("wa", None),
        P("wa"),
        P("wa", None),
        P("wa", None),
        P("wa", None),
    )
    return jax.shard_map(
        per_device, mesh=mesh, in_specs=in_specs, out_specs=out_specs, check_vma=False
    )
```
